256 devices in a mesh: gx: 64 (over z, y, core), gy: 4 (over x).
Axes of the slice: x: 4, y: 4, z: 8, core: 2. Of those that a mesh axis runs over, the one named last changes fastest.
Arguments:
- velocity_u: float32 [4096, 16, 2048], P('gx', None, 'gy'), may hold values from -6 to 6
- wall_strain: float32 [4096, 16, 2048], P('gx', None, 'gy'), may hold values from -6 to 6
- damping: float32 [16, 2048], P(None, 'gy'), may hold values from 0.88 to 1
Outputs:
- second_deriv: float32 [4096, 16, 2048], P('gx', None, 'gy')
- cosine_coeffs: float32 [4096, 16, 2048], P('gx', None, 'gy')
- pressure: float32 [4096, 16, 2048], P('gx', None, 'gy')
The draws below stay inside these ranges and needn't reach their ends.
All inputs are finite; a program needn't handle non-finite values.
Results may differ from the reference program's by a relative error of at most 0.0003.
Values sent between devices are 32-bit elements; how exact they have to be, the bound alone decides.
A program may use at most 128 MiB of HBM per device.

```python
import math
import jax
import jax.numpy as jnp
from jax import lax

NZ = 16
NY = 2048
NX = 4096


def draw_wall_strain(key, part):
    rough_key = jax.random.fold_in(key, 0)
    return jnp.clip(jax.random.normal(rough_key, (NX, NZ, NY), jnp.float32), -6.0, 6.0)


def draw_damping(key, part):
    choose_key, long_key, short_key = jax.random.split(key, 3)
    long_share = 0.5
    long_length = jnp.exp(jax.random.uniform(long_key, (NZ, NY), jnp.float32, math.log(0.45 * NX), math.log(0.9 * NX)))
    short_length = jnp.exp(jax.random.uniform(short_key, (NZ, NY), jnp.float32, math.log(8.0), math.log(0.45 * NX)))
    chosen = jax.random.uniform(choose_key, (NZ, NY), jnp.float32) < long_share
    length = jnp.where(chosen, long_length, short_length)
    return jnp.exp(-1.0 / length)


def level_of(stream_key, dims, cuts, least, top_value):
    gain = 1.0
    for dim, parts in cuts:
        steps = jax.random.uniform(jax.random.fold_in(jax.random.fold_in(stream_key, 6), dim), (parts,), jnp.float32, least / len(cuts), top_value / len(cuts))
        gain = gain * jnp.repeat(jnp.exp(steps), dims[dim] // parts).reshape((-1,) + (1,) * (len(dims) - 1 - dim))
    return gain


def centred(stream_key, shape, width, reach, cuts=(), kind=jnp.bfloat16):
    gain = level_of(stream_key, shape, cuts, -0.22, 0.18) if cuts else 1.0
    result = jax.random.normal(stream_key, shape, jnp.float32) * width * gain
    return jnp.minimum(jnp.maximum(result, -reach), reach).astype(kind)


def setup_inputs(seed: int = 0) -> dict:
    key_list = jax.random.split(jax.random.key(seed), 4)
    return {
        "velocity_u": centred(key_list[0], (NX, NZ, NY), 1.0, 6.0, ((0, 64), (2, 4)), jnp.float32),
        "wall_strain": draw_wall_strain(jax.random.fold_in(key_list[3], 71), 0),
        "damping": draw_damping(jax.random.fold_in(key_list[3], 71), 0),
    }


def reference(velocity_u, wall_strain, damping):
    padded = jnp.pad(velocity_u, ((3, 3), (0, 0), (0, 0)))

    def shifted(offset):
        return padded[3 + offset:3 + offset + NX]
    first_deriv = 0.75 * (shifted(1) - shifted(-1)) - 3.0 / 20.0 * (shifted(2) - shifted(-2)) + 1.0 / 60.0 * (shifted(3) - shifted(-3))
    second_deriv = 1.5 * (shifted(1) + shifted(-1)) - 3.0 / 20.0 * (shifted(2) + shifted(-2)) + 1.0 / 90.0 * (shifted(3) + shifted(-3)) - 49.0 / 18.0 * shifted(0)
    divergence = first_deriv + wall_strain
    samples = jnp.arange(NY, dtype=jnp.int32)
    phase = (samples[:, None] * 2 + 1) * samples[None, :] % (4 * NY)
    table = jnp.sqrt(jnp.float32(2.0 / NY)) * jnp.cos(jnp.float32(jnp.pi) * phase.astype(jnp.float32) / (2.0 * NY))
    flat = divergence.reshape(-1, NY)
    cosine_coeffs = jnp.dot(flat, table, precision=lax.Precision.HIGHEST, preferred_element_type=jnp.float32).reshape(divergence.shape)
    weight = ((1.0 - damping) * (1.0 + damping)) ** 1.5
    forcing = weight[None, :, :] * cosine_coeffs

    def forward_step(carry, row):
        value = row + damping * carry
        return (value, value)
    zeros_plane = jnp.zeros((NZ, NY), jnp.float32)
    _, forward_sum = lax.scan(forward_step, zeros_plane, forcing)

    def backward_step(carry, row):
        value = row + damping * carry
        return (value, value)
    _, pressure = lax.scan(backward_step, zeros_plane, forward_sum, reverse=True)
    return (second_deriv, cosine_coeffs, pressure)
```

```python
import functools
import math

import jax
import jax.numpy as jnp
import ml_dtypes
import numpy as np
from jax import lax
from jax.experimental import pallas as pl
from jax.experimental.pallas import tpu as pltpu
from jax.sharding import PartitionSpec as P

MESH = pl.DeviceIdType.MESH
NY = 2048
GY = 4
CELLS = 64
PLANES = 16
COLS = 512
OWN = CELLS // GY
ROUNDS = (1, 2, 0, 3)
STEP = OWN // len(ROUNDS)
F32 = jnp.float32
BF16 = jnp.bfloat16


@functools.cache
def cosine_tables():
    n = np.arange(NY, dtype=np.int64)
    phase = (2 * n[:, None] + 1) * n[None, :] % (4 * NY)
    table = math.sqrt(2.0 / NY) * np.cos(np.pi * phase.astype(np.float64) / (2.0 * NY))
    high = table.astype(ml_dtypes.bfloat16)
    low = (table - high.astype(np.float64)).astype(ml_dtypes.bfloat16)
    return high, low


def split(value):
    high = value.astype(BF16)
    return high, (value - high.astype(F32)).astype(BF16)


def responses(damping):
    power, gain = damping * damping, damping
    for s in range(9):
        gain = gain * (1.0 + power)
        if s == 5:
            block = gain
            power = power * power
            block_scale = None
        else:
            power = power * power
    scale = damping
    for _ in range(6):
        scale = scale * scale
    block_scale = scale
    for _ in range(3):
        scale = scale * scale
    return block_scale, scale, block, gain


def kernel(
    u, w, damping, high_hbm, low_hbm,
    second_out, coeffs_out, pressure_out,
    source, second, rows, modes, coeffs, forward, table_hi, table_lo, lhs,
    halo, lines, gathered, slabs, back, carried, small,
    halo_send, halo_recv, row_send, row_recv, mode_send, mode_recv,
    a_send, a_recv, b_send, b_recv, c_send, c_recv, table_sem, out_sem,
):
    gx, gy = lax.axis_index("gx"), lax.axis_index("gy")
    z, member = gx // 8, lax.rem(gx, 8)

    def over_gy(d):
        return {"gy": lax.rem(gy + d, GY)}

    def in_slab(d):
        return {"gx": z * 8 + lax.rem(member + d, 8)}

    def over_z(d):
        return {"gx": lax.rem(z + d, 8) * 8 + member}

    following, previous = {"gx": lax.rem(gx + 1, 64)}, {"gx": lax.rem(gx + 63, 64)}
    peers = [following, previous] + [over_gy(d) for d in range(1, GY)]
    peers += [in_slab(d) for d in range(1, 8)] + [over_z(d) for d in range(1, 8)]
    barrier = pltpu.get_barrier_semaphore()
    for peer in peers:
        pl.semaphore_signal(barrier, inc=1, device_id=peer, device_id_type=MESH)

    tables = []
    for d in range(GY):
        block = pl.ds(pl.multiple_of(lax.rem(gy + GY - d, GY) * COLS, COLS), COLS)
        here = pl.ds(d * COLS, COLS)
        tables.append(pltpu.make_async_copy(high_hbm.at[block], table_hi.at[here], table_sem.at[2 * d]))
        tables.append(pltpu.make_async_copy(low_hbm.at[block], table_lo.at[here], table_sem.at[2 * d + 1]))
    for copy in tables:
        copy.start()

    def stencil(at, i):
        m3, m2, m1, c, p1, p2, p3 = [at(k) for k in range(-3, 4)]
        first = 0.75 * (p1 - m1) - 0.15 * (p2 - m2) + (1.0 / 60.0) * (p3 - m3)
        source[i] = first + w[i]
        second[i] = 1.5 * (p1 + m1) - 0.15 * (p2 + m2) + (1.0 / 90.0) * (p3 + m3) - (49.0 / 18.0) * c

    def inside(i, carry):
        stencil(lambda k: u[i + k], i)
        return carry

    lax.fori_loop(3, CELLS - 3, inside, 0)

    pl.semaphore_wait(barrier, len(peers))

    def remote(src, dst, send, recv, peer):
        return pltpu.make_async_remote_copy(
            src_ref=src, dst_ref=dst, send_sem=send, recv_sem=recv, device_id=peer, device_id_type=MESH
        )

    halos = [
        remote(u.at[pl.ds(CELLS - 3, 3)], halo.at[0], halo_send.at[0], halo_recv.at[0], following),
        remote(u.at[pl.ds(0, 3)], halo.at[1], halo_send.at[1], halo_recv.at[1], previous),
    ]
    for copy in halos:
        copy.start()

    row_copies, mode_copies = {}, {}

    def send_rows(q):
        for d in range(1, GY):
            start = lax.rem(gy + d, GY) * OWN + q * STEP
            k = (d - 1) * len(ROUNDS) + q
            row_copies[d, q] = remote(
                source.at[pl.ds(start, STEP)], rows.at[d - 1, pl.ds(q * STEP, STEP)],
                row_send.at[k], row_recv.at[k], over_gy(d),
            )
            row_copies[d, q].start()

    send_rows(ROUNDS[0])
    send_rows(ROUNDS[1])
    for copy in halos:
        copy.wait()
    low_edge, high_edge = (gx > 0).astype(F32), (gx < 63).astype(F32)

    def edge(i):
        def at(k):
            j = i + k
            if j < 0:
                return halo[0, j + 3] * low_edge
            if j >= CELLS:
                return halo[1, j - CELLS] * high_edge
            return u[j]

        stencil(at, i)

    for i in (0, 1, 2, CELLS - 3, CELLS - 2, CELLS - 1):
        edge(i)
    send_rows(ROUNDS[2])
    send_rows(ROUNDS[3])
    second_copy = pltpu.make_async_copy(second, second_out, out_sem.at[0])
    second_copy.start()
    for copy in tables:
        copy.wait()

    height = STEP * PLANES

    def transform(q):
        for d in range(GY):
            if d:
                row_copies[d, q].wait_recv()
                part = rows[d - 1, q * STEP : (q + 1) * STEP]
            else:
                part = source[pl.ds(gy * OWN + q * STEP, STEP)]
            hi, lo = split(part.reshape(height, COLS))
            lhs[:height, d * COLS : (d + 1) * COLS] = hi
            lhs[height:, d * COLS : (d + 1) * COLS] = lo

        def columns(j, carry):
            at = pl.ds(pl.multiple_of(j * 256, 256), 256)
            both = jnp.dot(lhs[...], table_hi[:, at], preferred_element_type=F32)
            cross = jnp.dot(lhs[:height], table_lo[:, at], preferred_element_type=F32)
            total = both[:height] + both[height:] + cross
            modes[j // 2, q * STEP : (q + 1) * STEP, :, pl.ds(pl.multiple_of(lax.rem(j, 2) * 256, 256), 256)] = (
                total.reshape(STEP, PLANES, 256)
            )
            return carry

        lax.fori_loop(0, NY // 256, columns, 0)
        for d in range(1, GY):
            k = (d - 1) * len(ROUNDS) + q
            mode_copies[d, q] = remote(
                modes.at[lax.rem(gy + d, GY), pl.ds(q * STEP, STEP)],
                coeffs.at[pl.ds(gy * OWN + q * STEP, STEP)],
                mode_send.at[k], mode_recv.at[k], over_gy(d),
            )
            mode_copies[d, q].start()
        coeffs[pl.ds(gy * OWN + q * STEP, STEP)] = modes[gy, q * STEP : (q + 1) * STEP]

    for q in ROUNDS:
        transform(q)

    for q in ROUNDS:
        for d in range(1, GY):
            mode_copies[d, q].wait_recv()
    coeffs_copy = pltpu.make_async_copy(coeffs, coeffs_out, out_sem.at[1])
    coeffs_copy.start()

    lam = damping[...]
    v = (1.0 - lam) * (1.0 + lam)
    weight = v * jnp.sqrt(v)

    def ahead(i, value):
        value = weight * coeffs[i] + lam * value
        forward[i] = value
        return value

    def behind(i, value):
        return forward[CELLS - 1 - i] + lam * value

    zero = jnp.zeros((PLANES, COLS), F32)
    end = lax.fori_loop(0, CELLS, ahead, zero, unroll=4)
    start = lax.fori_loop(0, CELLS, behind, zero, unroll=4)

    def groups():
        for g in range(8):
            yield g, slice(8 * (g // 4), 8 * (g // 4) + 8), slice(128 * (g % 4), 128 * (g % 4) + 128)

    for g, sub, lane in groups():
        lines[g, 0] = end[sub, lane]
        lines[g, 1] = start[sub, lane]
        small[g] = lam[sub, lane]

    a_copies = []
    for d in range(1, 8):
        copy = remote(lines.at[lax.rem(member + d, 8)], gathered.at[member], a_send.at[d - 1], a_recv.at[d - 1], in_slab(d))
        copy.start()
        a_copies.append(copy)
    gathered[member] = lines[member]
    scale, slab_scale, answer, slab_answer = responses(small[member])
    for copy in a_copies:
        copy.wait()
    s_slab = jnp.zeros((8, 128), F32)
    seen = []
    for m in range(8):
        seen.append(s_slab)
        s_slab = scale * s_slab + gathered[m, 0]
    t_slab = jnp.zeros((8, 128), F32)
    for m in reversed(range(8)):
        t_slab = gathered[m, 1] + answer * seen[m] + scale * t_slab
    slabs[z, 0] = s_slab
    slabs[z, 1] = t_slab
    b_copies = []
    for d in range(1, 8):
        copy = remote(slabs.at[z], slabs.at[z], b_send.at[d - 1], b_recv.at[d - 1], over_z(d))
        copy.start()
        b_copies.append(copy)
    for copy in b_copies:
        copy.wait()
    f = jnp.zeros((8, 128), F32)
    seen = []
    for k in range(8):
        seen.append(f)
        small[8 + k] = f
        f = slab_scale * f + slabs[k, 0]
    p = jnp.zeros((8, 128), F32)
    for k in reversed(range(8)):
        small[16 + k] = p
        p = slabs[k, 1] + slab_answer * seen[k] + slab_scale * p
    f, p = small[8 + z], small[16 + z]
    seen = []
    for m in range(8):
        seen.append(f)
        back[m, 0] = f
        f = scale * f + gathered[m, 0]
    for m in reversed(range(8)):
        back[m, 1] = p
        p = gathered[m, 1] + answer * seen[m] + scale * p
    c_copies = []
    for d in range(1, 8):
        copy = remote(back.at[lax.rem(member + d, 8)], carried.at[member], c_send.at[d - 1], c_recv.at[d - 1], in_slab(d))
        copy.start()
        c_copies.append(copy)
    carried[member] = back[member]
    for copy in c_copies:
        copy.wait()

    def joined(which):
        halves = [jnp.concatenate([carried[4 * h + g, which] for g in range(4)], axis=1) for h in range(2)]
        return jnp.concatenate(halves, axis=0)

    lax.fori_loop(0, CELLS, ahead, joined(0), unroll=4)
    second_copy.wait()

    def final(i, value):
        k = CELLS - 1 - i
        value = forward[k] + lam * value
        second[k] = value
        return value

    lax.fori_loop(0, CELLS, final, joined(1), unroll=4)
    pressure_copy = pltpu.make_async_copy(second, pressure_out, out_sem.at[2])
    pressure_copy.start()
    for q in ROUNDS:
        for d in range(1, GY):
            row_copies[d, q].wait_send()
            mode_copies[d, q].wait_send()
    coeffs_copy.wait()
    pressure_copy.wait()


def body(velocity_u, wall_strain, damping):
    high, low = cosine_tables()
    block = (CELLS, PLANES, COLS)
    vmem = pl.BlockSpec(memory_space=pltpu.VMEM)
    anywhere = pl.BlockSpec(memory_space=pl.ANY)
    dma = pltpu.SemaphoreType.DMA
    n = 3 * len(ROUNDS)
    return pl.pallas_call(
        kernel,
        out_shape=[jax.ShapeDtypeStruct(block, F32)] * 3,
        in_specs=[vmem, vmem, vmem, anywhere, anywhere],
        out_specs=[anywhere] * 3,
        scratch_shapes=[
            pltpu.VMEM(block, F32),
            pltpu.VMEM(block, F32),
            pltpu.VMEM((GY - 1, OWN, PLANES, COLS), F32),
            pltpu.VMEM((GY, OWN, PLANES, COLS), F32),
            pltpu.VMEM(block, F32),
            pltpu.VMEM(block, F32),
            pltpu.VMEM((NY, NY), BF16),
            pltpu.VMEM((NY, NY), BF16),
            pltpu.VMEM((2 * STEP * PLANES, NY), BF16),
            pltpu.VMEM((2, 3, PLANES, COLS), F32),
            pltpu.VMEM((8, 2, 8, 128), F32),
            pltpu.VMEM((8, 2, 8, 128), F32),
            pltpu.VMEM((8, 2, 8, 128), F32),
            pltpu.VMEM((8, 2, 8, 128), F32),
            pltpu.VMEM((8, 2, 8, 128), F32),
            pltpu.VMEM((24, 8, 128), F32),
            dma((2,)), dma((2,)), dma((n,)), dma((n,)), dma((n,)), dma((n,)),
            dma((7,)), dma((7,)), dma((7,)), dma((7,)), dma((7,)), dma((7,)),
            dma((8,)), dma((3,)),
        ],
        compiler_params=pltpu.CompilerParams(
            collective_id=0, has_side_effects=True, vmem_limit_bytes=56 << 20
        ),
        name="channel",
    )(velocity_u, wall_strain, damping, jnp.asarray(high), jnp.asarray(low))


def solution(mesh):
    spec = P("gx", None, "gy")
    return jax.shard_map(
        body,
        mesh=mesh,
        in_specs=(spec, spec, P(None, "gy")),
        out_specs=(spec, spec, spec),
        check_vma=False,
    )
```

```python
import functools
import math

import jax
import jax.numpy as jnp
import ml_dtypes
import numpy as np
from jax import lax
from jax.experimental import pallas as pl
from jax.experimental.pallas import tpu as pltpu
from jax.sharding import PartitionSpec as P

MESH = pl.DeviceIdType.MESH
NY = 2048
GY = 4
CELLS = 64
PLANES = 16
COLS = 512
HALF = COLS // 2
OWN = CELLS // GY
ROUNDS = (1, 2, 0, 3)
STEP = OWN // len(ROUNDS)
PIECE = STEP // 2
F32 = jnp.float32
BF16 = jnp.bfloat16


@functools.cache
def cosine_tables():
    n = np.arange(NY, dtype=np.int64)
    phase = (2 * n[:, None] + 1) * n[None, :] % (4 * NY)
    table = math.sqrt(2.0 / NY) * np.cos(np.pi * phase.astype(np.float64) / (2.0 * NY))
    high = table.astype(ml_dtypes.bfloat16)
    low = (table - high.astype(np.float64)).astype(ml_dtypes.bfloat16)
    return high, low


def split(value):
    high = value.astype(BF16)
    return high, (value - high.astype(F32)).astype(BF16)


def response(damping, doublings):
    power, gain = damping * damping, damping * (1.0 + damping * damping)
    for _ in range(doublings - 1):
        power = power * power
        gain = gain * (1.0 + power)
    scale = damping
    for _ in range(doublings):
        scale = scale * scale
    return scale, gain


def weight_of(damping):
    v = (1.0 - damping) * (1.0 + damping)
    return v * jnp.sqrt(v)


def kernel(
    u_hbm, w_hbm, damping_hbm, high_hbm, low_hbm,
    second, coeffs, factors, carried,
    u, w, damping, source, rows, modes, table_hi, table_lo, lhs,
    halo, late_damping, partial, arrived, lines, gathered, slabs, back, small,
    load_sem, table_sem, halo_send, halo_recv, damp_send, damp_recv, row_send, row_recv,
    early_send, early_recv, late_send, late_recv, part_send, part_recv,
    a_send, a_recv, b_send, b_recv, c_send, c_recv,
):
    gx, gy = lax.axis_index("gx"), lax.axis_index("gy")
    z, member = gx // 8, lax.rem(gx, 8)

    def over_gy(d):
        return {"gy": lax.rem(gy + d, GY)}

    def in_slab(d):
        return {"gx": z * 8 + lax.rem(member + d, 8)}

    def over_z(d):
        return {"gx": lax.rem(z + d, 8) * 8 + member}

    following, previous = {"gx": lax.rem(gx + 1, 64)}, {"gx": lax.rem(gx + 63, 64)}
    peers = [following, previous] + [over_gy(d) for d in range(1, GY)]
    peers += [in_slab(d) for d in range(1, 8)] + [over_z(d) for d in range(1, 8)]
    barrier = pltpu.get_barrier_semaphore()
    for peer in peers:
        pl.semaphore_signal(barrier, inc=1, device_id=peer, device_id_type=MESH)

    loads = [
        pltpu.make_async_copy(u_hbm, u, load_sem.at[0]),
        pltpu.make_async_copy(w_hbm, w, load_sem.at[1]),
        pltpu.make_async_copy(damping_hbm, damping, load_sem.at[2]),
    ]
    tables = []
    for d in range(GY):
        block = pl.ds(pl.multiple_of(lax.rem(gy + GY - d, GY) * COLS, COLS), COLS)
        here = pl.ds(d * COLS, COLS)
        tables.append(pltpu.make_async_copy(high_hbm.at[block], table_hi.at[here], table_sem.at[2 * d]))
        tables.append(pltpu.make_async_copy(low_hbm.at[block], table_lo.at[here], table_sem.at[2 * d + 1]))
    for copy in loads + tables:
        copy.start()

    def remote(src, dst, send, recv, peer):
        return pltpu.make_async_remote_copy(
            src_ref=src, dst_ref=dst, send_sem=send, recv_sem=recv, device_id=peer, device_id_type=MESH
        )

    def stencil(at, i):
        m3, m2, m1, c, p1, p2, p3 = [at(k) for k in range(-3, 4)]
        first = 0.75 * (p1 - m1) - 0.15 * (p2 - m2) + (1.0 / 60.0) * (p3 - m3)
        source[i] = first + w[i]
        second[i] = 1.5 * (p1 + m1) - 0.15 * (p2 + m2) + (1.0 / 90.0) * (p3 + m3) - (49.0 / 18.0) * c

    def inside(first, last):
        def step(i, carry):
            stencil(lambda k: u[i + k], i)
            return carry

        lax.fori_loop(first, last, step, 0)

    def inner_chunk(q):
        for j in range(GY):
            inside(max(j * OWN + q * STEP, 3), min(j * OWN + q * STEP + STEP, CELLS - 3))

    row_copies, early_copies, late_copies = {}, {}, {}

    def send_rows(q):
        for half in range(2):
            at = q * STEP + half * PIECE
            for d in range(1, GY):
                k = ((d - 1) * len(ROUNDS) + q) * 2 + half
                copy = remote(
                    source.at[pl.ds(lax.rem(gy + d, GY) * OWN + at, PIECE)], rows.at[d - 1, pl.ds(at, PIECE)],
                    row_send.at[k], row_recv.at[k], over_gy(d),
                )
                copy.start()
                row_copies[d, q, half] = copy

    loads[0].wait()
    loads[1].wait()
    loads[2].wait()
    inner_chunk(ROUNDS[0])
    pl.semaphore_wait(barrier, len(peers))
    halos = [
        remote(u.at[pl.ds(CELLS - 3, 3)], halo.at[0], halo_send.at[0], halo_recv.at[0], following),
        remote(u.at[pl.ds(0, 3)], halo.at[1], halo_send.at[1], halo_recv.at[1], previous),
    ]
    for copy in halos:
        copy.start()
    send_rows(ROUNDS[0])
    inner_chunk(ROUNDS[1])
    send_rows(ROUNDS[1])
    damps = []
    for d in range(1, GY):
        copy = remote(
            damping.at[:, pl.ds(HALF, HALF)], late_damping.at[gy], damp_send.at[d - 1], damp_recv.at[d - 1], over_gy(d)
        )
        copy.start()
        damps.append(copy)
    late_damping[gy] = damping[:, HALF:]
    inner_chunk(ROUNDS[2])
    inner_chunk(ROUNDS[3])
    for copy in halos:
        copy.wait()
    low_edge, high_edge = (gx > 0).astype(F32), (gx < 63).astype(F32)

    def edge(i):
        def at(k):
            j = i + k
            if j < 0:
                return halo[0, j + 3] * low_edge
            if j >= CELLS:
                return halo[1, j - CELLS] * high_edge
            return u[j]

        stencil(at, i)

    for i in (0, 1, 2):
        edge(i)
    send_rows(ROUNDS[2])
    for i in (CELLS - 3, CELLS - 2, CELLS - 1):
        edge(i)
    send_rows(ROUNDS[3])

    lam = damping[...]
    factors[0] = lam
    factors[1] = weight_of(lam)
    for g in range(8):
        small[g] = lam[8 * (g // 4) : 8 * (g // 4) + 8, 128 * (g % 4) : 128 * (g % 4) + 128]
    scale, answer = response(small[member], 6)
    slab_scale, slab_answer = response(small[member], 9)
    sub_scale, sub_answer = response(lam[:, HALF:], 4)
    for copy in tables:
        copy.wait()

    height = STEP * PLANES

    def send_modes(q, late):
        copies, send, recv = (late_copies, late_send, late_recv) if late else (early_copies, early_send, early_recv)
        lanes = pl.ds(HALF if late else 0, HALF)
        for d in range(1, GY):
            k = (d - 1) * len(ROUNDS) + q
            copy = remote(
                modes.at[lax.rem(gy + d, GY), pl.ds(q * STEP, STEP), :, lanes],
                coeffs.at[pl.ds(gy * OWN + q * STEP, STEP), :, lanes],
                send.at[k], recv.at[k], over_gy(d),
            )
            copy.start()
            copies[d, q] = copy

    def transform(q):
        for d in range(GY):
            if d:
                row_copies[d, q, 0].wait_recv()
                row_copies[d, q, 1].wait_recv()
                part = rows[d - 1, q * STEP : (q + 1) * STEP]
            else:
                part = source[pl.ds(gy * OWN + q * STEP, STEP)]
            hi, lo = split(part.reshape(height, COLS))
            lhs[:height, d * COLS : (d + 1) * COLS] = hi
            lhs[height:, d * COLS : (d + 1) * COLS] = lo

        def columns(j, carry):
            at = pl.ds(pl.multiple_of(j * 256, 256), 256)
            both = jnp.dot(lhs[...], table_hi[:, at], preferred_element_type=F32)
            cross = jnp.dot(lhs[:height], table_lo[:, at], preferred_element_type=F32)
            total = both[:height] + both[height:] + cross
            modes[j // 2, q * STEP : (q + 1) * STEP, :, pl.ds(pl.multiple_of(lax.rem(j, 2) * 256, 256), 256)] = (
                total.reshape(STEP, PLANES, 256)
            )
            return carry

        lax.fori_loop(0, NY // 256, columns, 0, unroll=2)
        send_modes(q, False)
        coeffs[pl.ds(gy * OWN + q * STEP, STEP)] = modes[gy, q * STEP : (q + 1) * STEP]

    for q in ROUNDS:
        transform(q)

    for copy in damps:
        copy.wait()
    late = [late_damping[o] for o in range(GY)]
    late_weight = [weight_of(x) for x in late]
    blank = jnp.zeros((PLANES, HALF), F32)

    def own_rows(i, carry):
        found = []
        for o, (s, t, power) in enumerate(carry):
            s = late_weight[o] * modes[o, i, :, HALF:] + late[o] * s
            found.append((s, t + power * s, power * late[o]))
        return tuple(found)

    sums = lax.fori_loop(0, OWN, own_rows, ((blank, blank, blank + 1.0),) * GY)
    for o in range(GY):
        partial[o, 0] = sums[o][0]
        partial[o, 1] = sums[o][1]
    parts = []
    for d in range(1, GY):
        copy = remote(partial.at[lax.rem(gy + d, GY)], arrived.at[gy], part_send.at[d - 1], part_recv.at[d - 1], over_gy(d))
        copy.start()
        parts.append(copy)
    arrived[gy] = partial[gy]
    send_modes(ROUNDS[0], True)
    send_modes(ROUNDS[1], True)

    for q in ROUNDS:
        for d in range(1, GY):
            early_copies[d, q].wait_recv()
    first, first_weight = lam[:, :HALF], factors[1, :, :HALF]

    def all_rows(i, carry):
        s, t, power = carry
        s = first_weight * coeffs[i, :, :HALF] + first * s
        return s, t + power * s, power * first

    s_early, t_early, _ = lax.fori_loop(0, CELLS, all_rows, (blank, blank, blank + 1.0), unroll=4)
    for copy in parts:
        copy.wait()
    s_late, seen = blank, []
    for j in range(GY):
        seen.append(s_late)
        s_late = sub_scale * s_late + arrived[j, 0]
    t_late = blank
    for j in reversed(range(GY)):
        t_late = arrived[j, 1] + sub_answer * seen[j] + sub_scale * t_late
    for h in range(2):
        sub = slice(8 * h, 8 * h + 8)
        for g in range(2):
            lane = slice(128 * g, 128 * g + 128)
            lines[4 * h + g, 0] = s_early[sub, lane]
            lines[4 * h + g, 1] = t_early[sub, lane]
            lines[4 * h + 2 + g, 0] = s_late[sub, lane]
            lines[4 * h + 2 + g, 1] = t_late[sub, lane]

    a_copies = []
    for d in range(1, 8):
        copy = remote(lines.at[lax.rem(member + d, 8)], gathered.at[member], a_send.at[d - 1], a_recv.at[d - 1], in_slab(d))
        copy.start()
        a_copies.append(copy)
    gathered[member] = lines[member]
    send_modes(ROUNDS[2], True)
    for copy in a_copies:
        copy.wait()
    tile = jnp.zeros((8, 128), F32)
    s_slab, seen = tile, []
    for m in range(8):
        seen.append(s_slab)
        s_slab = scale * s_slab + gathered[m, 0]
    t_slab = tile
    for m in reversed(range(8)):
        t_slab = gathered[m, 1] + answer * seen[m] + scale * t_slab
    slabs[z, 0] = s_slab
    slabs[z, 1] = t_slab
    b_copies = []
    for d in range(1, 8):
        copy = remote(slabs.at[z], slabs.at[z], b_send.at[d - 1], b_recv.at[d - 1], over_z(d))
        copy.start()
        b_copies.append(copy)
    send_modes(ROUNDS[3], True)
    for copy in b_copies:
        copy.wait()
    f, seen = tile, []
    for k in range(8):
        seen.append(f)
        small[8 + k] = f
        f = slab_scale * f + slabs[k, 0]
    p = tile
    for k in reversed(range(8)):
        small[16 + k] = p
        p = slabs[k, 1] + slab_answer * seen[k] + slab_scale * p
    f, p = small[8 + z], small[16 + z]
    seen = []
    for m in range(8):
        seen.append(f)
        back[m, 0] = f
        f = scale * f + gathered[m, 0]
    for m in reversed(range(8)):
        back[m, 1] = p
        p = gathered[m, 1] + answer * seen[m] + scale * p
    c_copies = []
    for d in range(1, 8):
        copy = remote(back.at[lax.rem(member + d, 8)], carried.at[member], c_send.at[d - 1], c_recv.at[d - 1], in_slab(d))
        copy.start()
        c_copies.append(copy)
    carried[member] = back[member]
    for copy in c_copies:
        copy.wait()
    for q in ROUNDS:
        for d in range(1, GY):
            row_copies[d, q, 0].wait_send()
            row_copies[d, q, 1].wait_send()
            early_copies[d, q].wait_send()
            late_copies[d, q].wait()


def finish(second, coeffs, factors, carried, second_out, coeffs_out, pressure_out, forward, pressure, sem):
    whole = [
        pltpu.make_async_copy(coeffs, coeffs_out, sem.at[0]),
        pltpu.make_async_copy(second, second_out, sem.at[1]),
    ]
    for copy in whole:
        copy.start()
    lam, weight = factors[0], factors[1]

    def joined(which):
        halves = [jnp.concatenate([carried[4 * h + g, which] for g in range(4)], axis=1) for h in range(2)]
        return jnp.concatenate(halves, axis=0)

    def ahead(i, value):
        value = weight * coeffs[i] + lam * value
        forward[i] = value
        return value

    lax.fori_loop(0, CELLS, ahead, joined(0), unroll=4)
    value, quarter = joined(1), CELLS // 4
    for part in reversed(range(4)):

        def behind(i, value):
            k = (part + 1) * quarter - 1 - i
            value = forward[k] + lam * value
            pressure[k] = value
            return value

        value = lax.fori_loop(0, quarter, behind, value, unroll=4)
        here = pl.ds(part * quarter, quarter)
        copy = pltpu.make_async_copy(pressure.at[here], pressure_out.at[here], sem.at[2 + part])
        copy.start()
        whole.append(copy)
    for copy in whole:
        copy.wait()


def body(velocity_u, wall_strain, damping):
    high, low = (jnp.asarray(table) for table in cosine_tables())
    block, plane = (CELLS, PLANES, COLS), (PLANES, COLS)
    vmem = pl.BlockSpec(memory_space=pltpu.VMEM)
    anywhere = pl.BlockSpec(memory_space=pltpu.HBM)
    dma = pltpu.SemaphoreType.DMA
    n, groups = 3 * len(ROUNDS), (8, 2, 8, 128)
    between = pl.pallas_call(
        kernel,
        out_shape=[pltpu.VMEM(shape, F32) for shape in (block, block, (2, *plane), groups)],
        in_specs=[anywhere] * 5,
        out_specs=[vmem] * 4,
        scratch_shapes=[
            pltpu.VMEM(block, F32),
            pltpu.VMEM(block, F32),
            pltpu.VMEM(plane, F32),
            pltpu.VMEM(block, F32),
            pltpu.VMEM((GY - 1, OWN, PLANES, COLS), F32),
            pltpu.VMEM((GY, OWN, PLANES, COLS), F32),
            pltpu.VMEM((NY, NY), BF16),
            pltpu.VMEM((NY, NY), BF16),
            pltpu.VMEM((2 * STEP * PLANES, NY), BF16),
            pltpu.VMEM((2, 3, PLANES, COLS), F32),
            pltpu.VMEM((GY, PLANES, HALF), F32),
            pltpu.VMEM((GY, 2, PLANES, HALF), F32),
            pltpu.VMEM((GY, 2, PLANES, HALF), F32),
            pltpu.VMEM(groups, F32),
            pltpu.VMEM(groups, F32),
            pltpu.VMEM(groups, F32),
            pltpu.VMEM(groups, F32),
            pltpu.VMEM((24, 8, 128), F32),
            dma((3,)), dma((8,)), dma((2,)), dma((2,)), dma((3,)), dma((3,)), dma((2 * n,)), dma((2 * n,)),
            dma((n,)), dma((n,)), dma((n,)), dma((n,)), dma((3,)), dma((3,)),
            dma((7,)), dma((7,)), dma((7,)), dma((7,)), dma((7,)), dma((7,)),
        ],
        compiler_params=pltpu.CompilerParams(
            collective_id=0, has_side_effects=True, vmem_limit_bytes=40 << 20
        ),
        name="exchange",
    )(*[pltpu.with_memory_space_constraint(x, pltpu.HBM) for x in (velocity_u, wall_strain, damping, high, low)])
    return pl.pallas_call(
        finish,
        out_shape=[jax.ShapeDtypeStruct(block, F32)] * 3,
        in_specs=[vmem] * 4,
        out_specs=[anywhere] * 3,
        scratch_shapes=[pltpu.VMEM(block, F32), pltpu.VMEM(block, F32), dma((6,))],
        compiler_params=pltpu.CompilerParams(vmem_limit_bytes=16 << 20),
        name="finish",
    )(*between)


def solution(mesh):
    spec = P("gx", None, "gy")
    return jax.shard_map(
        body,
        mesh=mesh,
        in_specs=(spec, spec, P(None, "gy")),
        out_specs=(spec, spec, spec),
        check_vma=False,
    )
```

```python
import functools
import math

import jax
import jax.numpy as jnp
import ml_dtypes
import numpy as np
from jax import lax
from jax.experimental import pallas as pl
from jax.experimental.pallas import tpu as pltpu
from jax.sharding import PartitionSpec as P

MESH = pl.DeviceIdType.MESH
NY = 2048
GY = 4
CELLS = 64
PLANES = 16
COLS = 512
OWN = CELLS // GY
ROUNDS = (1, 2, 0, 3)
STEP = OWN // len(ROUNDS)
PIECE = STEP // 2
F32 = jnp.float32
BF16 = jnp.bfloat16


@functools.cache
def cosine_tables():
    n = np.arange(NY, dtype=np.int64)
    phase = (2 * n[:, None] + 1) * n[None, :] % (4 * NY)
    table = math.sqrt(2.0 / NY) * np.cos(np.pi * phase.astype(np.float64) / (2.0 * NY))
    high = table.astype(ml_dtypes.bfloat16)
    low = (table - high.astype(np.float64)).astype(ml_dtypes.bfloat16)
    return high, low


def split(value):
    high = value.astype(BF16)
    return high, (value - high.astype(F32)).astype(BF16)


def response(damping, doublings):
    power, gain = damping * damping, damping * (1.0 + damping * damping)
    for _ in range(doublings - 1):
        power = power * power
        gain = gain * (1.0 + power)
    scale = damping
    for _ in range(doublings):
        scale = scale * scale
    return scale, gain


def weight_of(damping):
    v = (1.0 - damping) * (1.0 + damping)
    return v * jnp.sqrt(v)


def kernel(
    u_hbm, w_hbm, damping_hbm, high_hbm, low_hbm,
    second, coeffs, factors, carried,
    u, w, damping, source, rows, modes, table_hi, table_lo, lhs,
    halo, all_damping, all_weight, sub, partial, arrived, lines, gathered, slabs, chain, back, small,
    load_sem, table_sem, halo_send, halo_recv, damp_send, damp_recv, row_send, row_recv, mode_send, mode_recv,
    part_send, part_recv, a_send, a_recv, b_send, b_recv, c_send, c_recv,
):
    gx, gy = lax.axis_index("gx"), lax.axis_index("gy")
    z, member = gx // 8, lax.rem(gx, 8)

    def over_gy(d):
        return {"gy": lax.rem(gy + d, GY)}

    def in_slab(d):
        return {"gx": z * 8 + lax.rem(member + d, 8)}

    above, below = {"gx": lax.rem(gx + 8, 64)}, {"gx": lax.rem(gx + 56, 64)}
    following, previous = {"gx": lax.rem(gx + 1, 64)}, {"gx": lax.rem(gx + 63, 64)}
    out_up, out_down = jnp.logical_and(member == 7, z < 7), jnp.logical_and(member == 0, z > 0)
    barrier = pltpu.get_barrier_semaphore()

    def greet(peer):
        pl.semaphore_signal(barrier, inc=1, device_id=peer, device_id_type=MESH)

    for d in range(1, GY):
        greet(over_gy(d))
    for d in range(1, 8):
        greet(in_slab(d))
    for needed, peer in ((z < 7, above), (z > 0, below), (out_up, following), (out_down, previous)):

        @pl.when(needed)
        def _(peer=peer):
            greet(peer)

    greeted = 10 + (z < 7).astype(jnp.int32) + (z > 0).astype(jnp.int32)
    greeted = greeted + out_up.astype(jnp.int32) + out_down.astype(jnp.int32)

    loads = [
        pltpu.make_async_copy(u_hbm, u, load_sem.at[0]),
        pltpu.make_async_copy(w_hbm, w, load_sem.at[1]),
        pltpu.make_async_copy(damping_hbm, damping, load_sem.at[2]),
    ]
    tables = []
    for d in range(GY):
        block = pl.ds(pl.multiple_of(lax.rem(gy + GY - d, GY) * COLS, COLS), COLS)
        here = pl.ds(d * COLS, COLS)
        tables.append(pltpu.make_async_copy(high_hbm.at[block], table_hi.at[here], table_sem.at[2 * d]))
        tables.append(pltpu.make_async_copy(low_hbm.at[block], table_lo.at[here], table_sem.at[2 * d + 1]))
    for copy in loads:
        copy.start()

    started = []

    def remote(src, dst, send, recv, peer):
        copy = pltpu.make_async_remote_copy(
            src_ref=src, dst_ref=dst, send_sem=send, recv_sem=recv, device_id=peer, device_id_type=MESH
        )
        copy.start()
        started.append(copy)
        return copy

    def stencil(at, i):
        m3, m2, m1, c, p1, p2, p3 = [at(k) for k in range(-3, 4)]
        first = 0.75 * (p1 - m1) - 0.15 * (p2 - m2) + (1.0 / 60.0) * (p3 - m3)
        source[i] = first + w[i]
        second[i] = 1.5 * (p1 + m1) - 0.15 * (p2 + m2) + (1.0 / 90.0) * (p3 + m3) - (49.0 / 18.0) * c

    def inner_chunk(q):
        def step(i, carry):
            stencil(lambda k: u[i + k], i)
            return carry

        for j in range(GY):
            lax.fori_loop(max(j * OWN + q * STEP, 3), min(j * OWN + q * STEP + STEP, CELLS - 3), step, 0)

    row_copies, mode_copies = {}, {}

    def send_rows(q):
        for half in range(2):
            at = q * STEP + half * PIECE
            for d in range(1, GY):
                k = ((d - 1) * len(ROUNDS) + q) * 2 + half
                src = source.at[pl.ds(lax.rem(gy + d, GY) * OWN + at, PIECE)]
                dst = rows.at[d - 1, pl.ds(at, PIECE)]
                row_copies[d, q, half] = remote(src, dst, row_send.at[k], row_recv.at[k], over_gy(d))

    def send_modes(q):
        for half in range(2):
            at = q * STEP + half * PIECE
            for d in range(1, GY):
                k = ((d - 1) * len(ROUNDS) + q) * 2 + half
                src = modes.at[lax.rem(gy + d, GY), pl.ds(at, PIECE)]
                dst = coeffs.at[pl.ds(gy * OWN + at, PIECE)]
                mode_copies[d, q, half] = remote(src, dst, mode_send.at[k], mode_recv.at[k], over_gy(d))

    height = STEP * PLANES

    def transform(q):
        for d in range(GY):
            if d:
                row_copies[d, q, 0].wait_recv()
                row_copies[d, q, 1].wait_recv()
                part = rows[d - 1, q * STEP : (q + 1) * STEP]
            else:
                part = source[pl.ds(gy * OWN + q * STEP, STEP)]
            hi, lo = split(part.reshape(height, COLS))
            lhs[:height, d * COLS : (d + 1) * COLS] = hi
            lhs[height:, d * COLS : (d + 1) * COLS] = lo

        def columns(j, carry):
            at = pl.ds(pl.multiple_of(j * 256, 256), 256)
            both = jnp.dot(lhs[...], table_hi[:, at], preferred_element_type=F32)
            cross = jnp.dot(lhs[:height], table_lo[:, at], preferred_element_type=F32)
            total = both[:height] + both[height:] + cross
            modes[j // 2, q * STEP : (q + 1) * STEP, :, pl.ds(pl.multiple_of(lax.rem(j, 2) * 256, 256), 256)] = (
                total.reshape(STEP, PLANES, 256)
            )
            return carry

        lax.fori_loop(0, NY // 256, columns, 0, unroll=2)
        coeffs[pl.ds(gy * OWN + q * STEP, STEP)] = modes[gy, q * STEP : (q + 1) * STEP]

    r0, r1, r2, r3 = ROUNDS
    loads[0].wait()
    loads[1].wait()
    loads[2].wait()
    for copy in tables:
        copy.start()
    inner_chunk(r0)
    pl.semaphore_wait(barrier, greeted)

    def halo_copy(k):
        src = u.at[pl.ds((CELLS - 3) * (1 - k), 3)]
        peer = (following, previous)[k]
        return pltpu.make_async_remote_copy(
            src_ref=src, dst_ref=halo.at[k], send_sem=halo_send.at[k], recv_sem=halo_recv.at[k],
            device_id=peer, device_id_type=MESH,
        )

    has_next, has_previous = gx < 63, gx > 0

    @pl.when(has_next)
    def _():
        halo_copy(0).start()

    @pl.when(has_previous)
    def _():
        halo_copy(1).start()

    send_rows(r0)
    inner_chunk(r1)
    send_rows(r1)
    damps = [
        remote(damping, all_damping.at[gy], damp_send.at[d - 1], damp_recv.at[d - 1], over_gy(d)) for d in range(1, GY)
    ]
    all_damping[gy] = damping[...]
    inner_chunk(r2)
    inner_chunk(r3)

    @pl.when(has_previous)
    def _():
        halo_copy(0).wait_recv()
        halo_copy(1).wait_send()

    @pl.when(jnp.logical_not(has_previous))
    def _():
        halo[0] = jnp.zeros((3, PLANES, COLS), F32)

    @pl.when(has_next)
    def _():
        halo_copy(1).wait_recv()
        halo_copy(0).wait_send()

    @pl.when(jnp.logical_not(has_next))
    def _():
        halo[1] = jnp.zeros((3, PLANES, COLS), F32)

    def edge(i):
        def at(k):
            j = i + k
            if j < 0:
                return halo[0, j + 3]
            if j >= CELLS:
                return halo[1, j - CELLS]
            return u[j]

        stencil(at, i)

    for i in (0, 1, 2):
        edge(i)
    send_rows(r2)
    for i in (CELLS - 3, CELLS - 2, CELLS - 1):
        edge(i)
    send_rows(r3)

    lam = damping[...]
    factors[0] = lam
    factors[1] = weight_of(lam)
    for g in range(8):
        small[g] = lam[8 * (g // 4) : 8 * (g // 4) + 8, 128 * (g % 4) : 128 * (g % 4) + 128]
    for k, value in enumerate(response(lam, 4)):
        sub[k] = value
    for k, value in enumerate((*response(small[member], 6), *response(small[member], 9))):
        small[8 + k] = value
    for copy in damps:
        copy.wait_recv()
    for o in range(GY):
        all_weight[o] = weight_of(all_damping[o])
    for copy in tables:
        copy.wait()

    transform(r0)
    send_modes(r0)
    transform(r1)
    transform(r2)
    transform(r3)

    blank = jnp.zeros((PLANES, COLS), F32)
    for o in range(GY):

        def own_rows(i, carry, o=o):
            s, t, power = carry
            s = all_weight[o] * modes[o, i] + all_damping[o] * s
            return s, t + power * s, power * all_damping[o]

        s, t, _ = lax.fori_loop(0, OWN, own_rows, (blank, blank, blank + 1.0), unroll=2)
        partial[o, 0] = s
        partial[o, 1] = t
    parts = [
        remote(
            partial.at[lax.rem(gy + d, GY)], arrived.at[gy], part_send.at[d - 1], part_recv.at[d - 1],
            over_gy(d),
        )
        for d in range(1, GY)
    ]
    arrived[gy] = partial[gy]
    send_modes(r1)
    send_modes(r2)

    for copy in parts:
        copy.wait_recv()
    s, seen = blank, []
    for j in range(GY):
        seen.append(s)
        s = sub[0] * s + arrived[j, 0]
    t = blank
    for j in reversed(range(GY)):
        t = arrived[j, 1] + sub[1] * seen[j] + sub[0] * t
    for g in range(8):
        at = slice(8 * (g // 4), 8 * (g // 4) + 8), slice(128 * (g % 4), 128 * (g % 4) + 128)
        lines[g, 0] = s[at]
        lines[g, 1] = t[at]

    a_copies = [
        remote(lines.at[lax.rem(member + d, 8)], gathered.at[member], a_send.at[d - 1], a_recv.at[d - 1], in_slab(d))
        for d in range(1, 8)
    ]
    gathered[member] = lines[member]
    send_modes(r3)
    for copy in a_copies:
        copy.wait_recv()
    scale, answer, slab_scale, slab_answer = [small[8 + k] for k in range(4)]
    tile = jnp.zeros((8, 128), F32)
    s_slab, seen = tile, []
    for m in range(8):
        seen.append(s_slab)
        s_slab = scale * s_slab + gathered[m, 0]
    t_slab = tile
    for m in reversed(range(8)):
        t_slab = gathered[m, 1] + answer * seen[m] + scale * t_slab
    slabs[1] = jnp.zeros((3, 8, 128), F32)

    def up():
        return pltpu.make_async_remote_copy(
            src_ref=slabs.at[0, pl.ds(0, 1)], dst_ref=chain.at[pl.ds(0, 1)], send_sem=b_send.at[0],
            recv_sem=b_recv.at[0], device_id=above, device_id_type=MESH,
        )

    def down():
        return pltpu.make_async_remote_copy(
            src_ref=slabs.at[0, pl.ds(1, 2)], dst_ref=chain.at[pl.ds(1, 2)], send_sem=b_send.at[1],
            recv_sem=b_recv.at[1], device_id=below, device_id_type=MESH,
        )

    def pass_up():
        @pl.when(z > 0)
        def _():
            up().wait_recv()
            slabs[1, 0] = chain[0]

        slabs[0, 0] = s_slab + slab_scale * slabs[1, 0]

        @pl.when(z < 7)
        def _():
            up().start()

    def pass_down():
        @pl.when(z < 7)
        def _():
            down().wait_recv()
            slabs[1, 1] = chain[1]
            slabs[1, 2] = chain[2]

        slabs[0, 1] = t_slab + slab_scale * (slabs[1, 1] + slabs[1, 2] * s_slab)
        slabs[0, 2] = slab_answer + slab_scale * slab_scale * slabs[1, 2]

        @pl.when(z > 0)
        def _():
            down().start()

    @pl.when(z < 4)
    def _():
        pass_up()
        pass_down()

    @pl.when(z >= 4)
    def _():
        pass_down()
        pass_up()

    f = slabs[1, 0]
    p = slabs[1, 1] + slabs[1, 2] * (s_slab + slab_scale * f)
    seen = []
    for m in range(8):
        seen.append(f)
        back[m, 0] = f
        f = scale * f + gathered[m, 0]
    for m in reversed(range(8)):
        back[m, 1] = p
        p = gathered[m, 1] + answer * seen[m] + scale * p
    c_copies = [
        remote(back.at[lax.rem(member + d, 8)], carried.at[member], c_send.at[d - 1], c_recv.at[d - 1], in_slab(d))
        for d in range(1, 8)
    ]
    carried[member] = back[member]
    for copy in c_copies:
        copy.wait_recv()
    for copy in mode_copies.values():
        copy.wait_recv()

    @pl.when(z < 7)
    def _():
        up().wait_send()

    @pl.when(z > 0)
    def _():
        down().wait_send()

    for copy in started:
        copy.wait_send()


def finish(second, coeffs, factors, carried, second_out, coeffs_out, pressure_out, forward, pressure, sem):
    whole = [
        pltpu.make_async_copy(coeffs, coeffs_out, sem.at[0]),
        pltpu.make_async_copy(second, second_out, sem.at[1]),
    ]
    for copy in whole:
        copy.start()
    lam, weight = factors[0], factors[1]

    def joined(which):
        halves = [jnp.concatenate([carried[4 * h + g, which] for g in range(4)], axis=1) for h in range(2)]
        return jnp.concatenate(halves, axis=0)

    def ahead(i, value):
        value = weight * coeffs[i] + lam * value
        forward[i] = value
        return value

    lax.fori_loop(0, CELLS, ahead, joined(0), unroll=4)
    value, quarter = joined(1), CELLS // 4
    for part in reversed(range(4)):

        def behind(i, value):
            k = (part + 1) * quarter - 1 - i
            value = forward[k] + lam * value
            pressure[k] = value
            return value

        value = lax.fori_loop(0, quarter, behind, value, unroll=4)
        here = pl.ds(part * quarter, quarter)
        copy = pltpu.make_async_copy(pressure.at[here], pressure_out.at[here], sem.at[2 + part])
        copy.start()
        whole.append(copy)
    for copy in whole:
        copy.wait()


def body(velocity_u, wall_strain, damping):
    high, low = (jnp.asarray(table) for table in cosine_tables())
    block, plane = (CELLS, PLANES, COLS), (PLANES, COLS)
    vmem = pl.BlockSpec(memory_space=pltpu.VMEM)
    anywhere = pl.BlockSpec(memory_space=pltpu.HBM)
    dma = pltpu.SemaphoreType.DMA
    n, groups = 6 * len(ROUNDS), (8, 2, 8, 128)
    between = pl.pallas_call(
        kernel,
        out_shape=[pltpu.VMEM(shape, F32) for shape in (block, block, (2, *plane), groups)],
        in_specs=[anywhere] * 5,
        out_specs=[vmem] * 4,
        scratch_shapes=[
            pltpu.VMEM(block, F32),
            pltpu.VMEM(block, F32),
            pltpu.VMEM(plane, F32),
            pltpu.VMEM(block, F32),
            pltpu.VMEM((GY - 1, OWN, *plane), F32),
            pltpu.VMEM((GY, OWN, *plane), F32),
            pltpu.VMEM((NY, NY), BF16),
            pltpu.VMEM((NY, NY), BF16),
            pltpu.VMEM((2 * STEP * PLANES, NY), BF16),
            pltpu.VMEM((2, 3, *plane), F32),
            pltpu.VMEM((GY, *plane), F32),
            pltpu.VMEM((GY, *plane), F32),
            pltpu.VMEM((2, *plane), F32),
            pltpu.VMEM((GY, 2, *plane), F32),
            pltpu.VMEM((GY, 2, *plane), F32),
            pltpu.VMEM(groups, F32),
            pltpu.VMEM(groups, F32),
            pltpu.VMEM((2, 3, 8, 128), F32),
            pltpu.VMEM((3, 8, 128), F32),
            pltpu.VMEM(groups, F32),
            pltpu.VMEM((12, 8, 128), F32),
            dma((3,)), dma((8,)), dma((2,)), dma((2,)), dma((3,)), dma((3,)),
            dma((n,)), dma((n,)), dma((n,)), dma((n,)), dma((3,)), dma((3,)),
            dma((7,)), dma((7,)), dma((2,)), dma((2,)), dma((7,)), dma((7,)),
        ],
        compiler_params=pltpu.CompilerParams(
            collective_id=0, has_side_effects=True, vmem_limit_bytes=40 << 20
        ),
        name="exchange",
    )(*[pltpu.with_memory_space_constraint(x, pltpu.HBM) for x in (velocity_u, wall_strain, damping, high, low)])
    return pl.pallas_call(
        finish,
        out_shape=[jax.ShapeDtypeStruct(block, F32)] * 3,
        in_specs=[vmem] * 4,
        out_specs=[anywhere] * 3,
        scratch_shapes=[pltpu.VMEM(block, F32), pltpu.VMEM(block, F32), dma((6,))],
        compiler_params=pltpu.CompilerParams(vmem_limit_bytes=16 << 20),
        name="finish",
    )(*between)


def solution(mesh):
    spec = P("gx", None, "gy")
    return jax.shard_map(
        body,
        mesh=mesh,
        in_specs=(spec, spec, P(None, "gy")),
        out_specs=(spec, spec, spec),
        check_vma=False,
    )
```

```python
import functools
import math

import jax
import jax.numpy as jnp
import ml_dtypes
import numpy as np
from jax import lax
from jax.experimental import pallas as pl
from jax.experimental.pallas import tpu as pltpu
from jax.sharding import PartitionSpec as P

MESH = pl.DeviceIdType.MESH
NY = 2048
GY = 4
CELLS = 64
PLANES = 16
COLS = 512
OWN = CELLS // GY
ROUNDS = (1, 2, 0, 3)
STEP = OWN // len(ROUNDS)
PIECE = STEP // 2
F32 = jnp.float32
BF16 = jnp.bfloat16


@functools.cache
def cosine_tables():
    n = np.arange(NY, dtype=np.int64)
    phase = (2 * n[:, None] + 1) * n[None, :] % (4 * NY)
    table = math.sqrt(2.0 / NY) * np.cos(np.pi * phase.astype(np.float64) / (2.0 * NY))
    high = table.astype(ml_dtypes.bfloat16)
    low = (table - high.astype(np.float64)).astype(ml_dtypes.bfloat16)
    return high, low


def split(value):
    high = value.astype(BF16)
    return high, (value - high.astype(F32)).astype(BF16)


def response(damping, doublings):
    power, gain = damping * damping, damping * (1.0 + damping * damping)
    for _ in range(doublings - 1):
        power = power * power
        gain = gain * (1.0 + power)
    scale = damping
    for _ in range(doublings):
        scale = scale * scale
    return scale, gain


def weight_of(damping):
    v = (1.0 - damping) * (1.0 + damping)
    return v * jnp.sqrt(v)


def kernel(
    u_hbm, w_hbm, damping_hbm, high_hbm, low_hbm,
    second, coeffs, factors, carried,
    u, w, damping, source, rows, modes, table_hi, table_lo, lhs,
    halo, all_damping, all_weight, sub, partial, arrived, lines, gathered, slabs, back, small,
    load_sem, table_sem, halo_send, halo_recv, damp_send, damp_recv, row_send, row_recv, mode_send, mode_recv,
    part_send, part_recv, a_send, a_recv, b_send, b_recv, c_send, c_recv,
):
    gx, gy = lax.axis_index("gx"), lax.axis_index("gy")
    z, member = gx // 8, lax.rem(gx, 8)

    def over_gy(d):
        return {"gy": lax.rem(gy + d, GY)}

    def in_slab(d):
        return {"gx": z * 8 + lax.rem(member + d, 8)}

    def over_z(d):
        return {"gx": lax.rem(z + d, 8) * 8 + member}

    following, previous = {"gx": lax.rem(gx + 1, 64)}, {"gx": lax.rem(gx + 63, 64)}
    out_up, out_down = jnp.logical_and(member == 7, z < 7), jnp.logical_and(member == 0, z > 0)
    barrier = pltpu.get_barrier_semaphore()

    def greet(peer):
        pl.semaphore_signal(barrier, inc=1, device_id=peer, device_id_type=MESH)

    for d in range(1, GY):
        greet(over_gy(d))
    for d in range(1, 8):
        greet(in_slab(d))
    for d in range(1, 8):
        greet(over_z(d))
    for needed, peer in ((out_up, following), (out_down, previous)):

        @pl.when(needed)
        def _(peer=peer):
            greet(peer)

    greeted = 17 + out_up.astype(jnp.int32) + out_down.astype(jnp.int32)

    loads = [
        pltpu.make_async_copy(u_hbm, u, load_sem.at[0]),
        pltpu.make_async_copy(w_hbm, w, load_sem.at[1]),
        pltpu.make_async_copy(damping_hbm, damping, load_sem.at[2]),
    ]
    tables = []
    for d in range(GY):
        block = pl.ds(pl.multiple_of(lax.rem(gy + GY - d, GY) * COLS, COLS), COLS)
        here = pl.ds(d * COLS, COLS)
        tables.append(pltpu.make_async_copy(high_hbm.at[block], table_hi.at[here], table_sem.at[2 * d]))
        tables.append(pltpu.make_async_copy(low_hbm.at[block], table_lo.at[here], table_sem.at[2 * d + 1]))
    for copy in loads:
        copy.start()

    started = []

    def remote(src, dst, send, recv, peer):
        copy = pltpu.make_async_remote_copy(
            src_ref=src, dst_ref=dst, send_sem=send, recv_sem=recv, device_id=peer, device_id_type=MESH
        )
        copy.start()
        started.append(copy)
        return copy

    def stencil(at, i):
        m3, m2, m1, c, p1, p2, p3 = [at(k) for k in range(-3, 4)]
        first = 0.75 * (p1 - m1) - 0.15 * (p2 - m2) + (1.0 / 60.0) * (p3 - m3)
        source[i] = first + w[i]
        second[i] = 1.5 * (p1 + m1) - 0.15 * (p2 + m2) + (1.0 / 90.0) * (p3 + m3) - (49.0 / 18.0) * c

    def inner_chunk(q):
        def step(i, carry):
            stencil(lambda k: u[i + k], i)
            return carry

        for j in range(GY):
            lax.fori_loop(max(j * OWN + q * STEP, 3), min(j * OWN + q * STEP + STEP, CELLS - 3), step, 0)

    row_copies, mode_copies = {}, {}

    def send_rows(q):
        for half in range(2):
            at = q * STEP + half * PIECE
            for d in range(1, GY):
                k = ((d - 1) * len(ROUNDS) + q) * 2 + half
                src = source.at[pl.ds(lax.rem(gy + d, GY) * OWN + at, PIECE)]
                dst = rows.at[d - 1, pl.ds(at, PIECE)]
                row_copies[d, q, half] = remote(src, dst, row_send.at[k], row_recv.at[k], over_gy(d))

    def send_modes(q):
        for half in range(2):
            at = q * STEP + half * PIECE
            for d in range(1, GY):
                k = ((d - 1) * len(ROUNDS) + q) * 2 + half
                src = modes.at[lax.rem(gy + d, GY), pl.ds(at, PIECE)]
                dst = coeffs.at[pl.ds(gy * OWN + at, PIECE)]
                mode_copies[d, q, half] = remote(src, dst, mode_send.at[k], mode_recv.at[k], over_gy(d))

    height = STEP * PLANES

    def transform(q):
        for d in range(GY):
            if d:
                row_copies[d, q, 0].wait_recv()
                row_copies[d, q, 1].wait_recv()
                part = rows[d - 1, q * STEP : (q + 1) * STEP]
            else:
                part = source[pl.ds(gy * OWN + q * STEP, STEP)]
            hi, lo = split(part.reshape(height, COLS))
            lhs[:height, d * COLS : (d + 1) * COLS] = hi
            lhs[height:, d * COLS : (d + 1) * COLS] = lo

        def columns(j, carry):
            at = pl.ds(pl.multiple_of(j * 256, 256), 256)
            both = jnp.dot(lhs[...], table_hi[:, at], preferred_element_type=F32)
            cross = jnp.dot(lhs[:height], table_lo[:, at], preferred_element_type=F32)
            total = both[:height] + both[height:] + cross
            modes[j // 2, q * STEP : (q + 1) * STEP, :, pl.ds(pl.multiple_of(lax.rem(j, 2) * 256, 256), 256)] = (
                total.reshape(STEP, PLANES, 256)
            )
            return carry

        lax.fori_loop(0, NY // 256, columns, 0, unroll=2)
        coeffs[pl.ds(gy * OWN + q * STEP, STEP)] = modes[gy, q * STEP : (q + 1) * STEP]

    r0, r1, r2, r3 = ROUNDS
    loads[0].wait()
    loads[1].wait()
    loads[2].wait()
    for copy in tables:
        copy.start()
    inner_chunk(r0)
    pl.semaphore_wait(barrier, greeted)

    def halo_copy(k):
        src = u.at[pl.ds((CELLS - 3) * (1 - k), 3)]
        peer = (following, previous)[k]
        return pltpu.make_async_remote_copy(
            src_ref=src, dst_ref=halo.at[k], send_sem=halo_send.at[k], recv_sem=halo_recv.at[k],
            device_id=peer, device_id_type=MESH,
        )

    has_next, has_previous = gx < 63, gx > 0

    @pl.when(has_next)
    def _():
        halo_copy(0).start()

    @pl.when(has_previous)
    def _():
        halo_copy(1).start()

    send_rows(r0)
    inner_chunk(r1)
    send_rows(r1)
    damps = [
        remote(damping, all_damping.at[gy], damp_send.at[d - 1], damp_recv.at[d - 1], over_gy(d)) for d in range(1, GY)
    ]
    all_damping[gy] = damping[...]
    inner_chunk(r2)
    inner_chunk(r3)

    @pl.when(has_previous)
    def _():
        halo_copy(0).wait_recv()
        halo_copy(1).wait_send()

    @pl.when(jnp.logical_not(has_previous))
    def _():
        halo[0] = jnp.zeros((3, PLANES, COLS), F32)

    @pl.when(has_next)
    def _():
        halo_copy(1).wait_recv()
        halo_copy(0).wait_send()

    @pl.when(jnp.logical_not(has_next))
    def _():
        halo[1] = jnp.zeros((3, PLANES, COLS), F32)

    def edge(i):
        def at(k):
            j = i + k
            if j < 0:
                return halo[0, j + 3]
            if j >= CELLS:
                return halo[1, j - CELLS]
            return u[j]

        stencil(at, i)

    for i in (0, 1, 2):
        edge(i)
    send_rows(r2)
    for i in (CELLS - 3, CELLS - 2, CELLS - 1):
        edge(i)
    send_rows(r3)

    lam = damping[...]
    factors[0] = lam
    factors[1] = weight_of(lam)
    for g in range(8):
        small[g] = lam[8 * (g // 4) : 8 * (g // 4) + 8, 128 * (g % 4) : 128 * (g % 4) + 128]
    for k, value in enumerate(response(lam, 4)):
        sub[k] = value
    for k, value in enumerate((*response(small[member], 6), *response(small[member], 9))):
        small[8 + k] = value
    for copy in damps:
        copy.wait_recv()
    for o in range(GY):
        all_weight[o] = weight_of(all_damping[o])
    for copy in tables:
        copy.wait()

    transform(r0)
    send_modes(r0)
    transform(r1)
    transform(r2)
    transform(r3)

    blank = jnp.zeros((PLANES, COLS), F32)
    for o in range(GY):

        def own_rows(i, carry, o=o):
            s, t, power = carry
            s = all_weight[o] * modes[o, i] + all_damping[o] * s
            return s, t + power * s, power * all_damping[o]

        s, t, _ = lax.fori_loop(0, OWN, own_rows, (blank, blank, blank + 1.0), unroll=2)
        partial[o, 0] = s
        partial[o, 1] = t
    parts = [
        remote(
            partial.at[lax.rem(gy + d, GY)], arrived.at[gy], part_send.at[d - 1], part_recv.at[d - 1],
            over_gy(d),
        )
        for d in range(1, GY)
    ]
    arrived[gy] = partial[gy]
    send_modes(r1)
    send_modes(r2)

    for copy in parts:
        copy.wait_recv()
    s, seen = blank, []
    for j in range(GY):
        seen.append(s)
        s = sub[0] * s + arrived[j, 0]
    t = blank
    for j in reversed(range(GY)):
        t = arrived[j, 1] + sub[1] * seen[j] + sub[0] * t
    for g in range(8):
        at = slice(8 * (g // 4), 8 * (g // 4) + 8), slice(128 * (g % 4), 128 * (g % 4) + 128)
        lines[g, 0] = s[at]
        lines[g, 1] = t[at]

    a_copies = [
        remote(lines.at[lax.rem(member + d, 8)], gathered.at[member], a_send.at[d - 1], a_recv.at[d - 1], in_slab(d))
        for d in range(1, 8)
    ]
    gathered[member] = lines[member]
    send_modes(r3)
    for copy in a_copies:
        copy.wait_recv()
    scale, answer, slab_scale, slab_answer = [small[8 + k] for k in range(4)]
    tile = jnp.zeros((8, 128), F32)
    s_slab, seen = tile, []
    for m in range(8):
        seen.append(s_slab)
        s_slab = scale * s_slab + gathered[m, 0]
    t_slab = tile
    for m in reversed(range(8)):
        t_slab = gathered[m, 1] + answer * seen[m] + scale * t_slab
    slabs[z, 0] = s_slab
    slabs[z, 1] = t_slab
    b_copies = [
        remote(slabs.at[z], slabs.at[z], b_send.at[d - 1], b_recv.at[d - 1], over_z(d)) for d in range(1, 8)
    ]
    for copy in b_copies:
        copy.wait_recv()
    f, seen = tile, []
    for k in range(8):
        seen.append(f)
        small[12 + k] = f
        f = slab_scale * f + slabs[k, 0]
    p = tile
    for k in reversed(range(8)):
        small[20 + k] = p
        p = slabs[k, 1] + slab_answer * seen[k] + slab_scale * p
    f, p = small[12 + z], small[20 + z]
    seen = []
    for m in range(8):
        seen.append(f)
        back[m, 0] = f
        f = scale * f + gathered[m, 0]
    for m in reversed(range(8)):
        back[m, 1] = p
        p = gathered[m, 1] + answer * seen[m] + scale * p
    c_copies = [
        remote(back.at[lax.rem(member + d, 8)], carried.at[member], c_send.at[d - 1], c_recv.at[d - 1], in_slab(d))
        for d in range(1, 8)
    ]
    carried[member] = back[member]
    for copy in c_copies:
        copy.wait_recv()
    for copy in mode_copies.values():
        copy.wait_recv()

    for copy in started:
        copy.wait_send()


def finish(second, coeffs, factors, carried, second_out, coeffs_out, pressure_out, forward, pressure, sem):
    whole = [
        pltpu.make_async_copy(coeffs, coeffs_out, sem.at[0]),
        pltpu.make_async_copy(second, second_out, sem.at[1]),
    ]
    for copy in whole:
        copy.start()
    lam, weight = factors[0], factors[1]

    def joined(which):
        halves = [jnp.concatenate([carried[4 * h + g, which] for g in range(4)], axis=1) for h in range(2)]
        return jnp.concatenate(halves, axis=0)

    def ahead(i, value):
        value = weight * coeffs[i] + lam * value
        forward[i] = value
        return value

    lax.fori_loop(0, CELLS, ahead, joined(0), unroll=4)
    value, quarter = joined(1), CELLS // 4
    for part in reversed(range(4)):

        def behind(i, value):
            k = (part + 1) * quarter - 1 - i
            value = forward[k] + lam * value
            pressure[k] = value
            return value

        value = lax.fori_loop(0, quarter, behind, value, unroll=4)
        here = pl.ds(part * quarter, quarter)
        copy = pltpu.make_async_copy(pressure.at[here], pressure_out.at[here], sem.at[2 + part])
        copy.start()
        whole.append(copy)
    for copy in whole:
        copy.wait()


def body(velocity_u, wall_strain, damping):
    high, low = (jnp.asarray(table) for table in cosine_tables())
    block, plane = (CELLS, PLANES, COLS), (PLANES, COLS)
    vmem = pl.BlockSpec(memory_space=pltpu.VMEM)
    anywhere = pl.BlockSpec(memory_space=pltpu.HBM)
    dma = pltpu.SemaphoreType.DMA
    n, groups = 6 * len(ROUNDS), (8, 2, 8, 128)
    between = pl.pallas_call(
        kernel,
        out_shape=[pltpu.VMEM(shape, F32) for shape in (block, block, (2, *plane), groups)],
        in_specs=[anywhere] * 5,
        out_specs=[vmem] * 4,
        scratch_shapes=[
            pltpu.VMEM(block, F32),
            pltpu.VMEM(block, F32),
            pltpu.VMEM(plane, F32),
            pltpu.VMEM(block, F32),
            pltpu.VMEM((GY - 1, OWN, *plane), F32),
            pltpu.VMEM((GY, OWN, *plane), F32),
            pltpu.VMEM((NY, NY), BF16),
            pltpu.VMEM((NY, NY), BF16),
            pltpu.VMEM((2 * STEP * PLANES, NY), BF16),
            pltpu.VMEM((2, 3, *plane), F32),
            pltpu.VMEM((GY, *plane), F32),
            pltpu.VMEM((GY, *plane), F32),
            pltpu.VMEM((2, *plane), F32),
            pltpu.VMEM((GY, 2, *plane), F32),
            pltpu.VMEM((GY, 2, *plane), F32),
            pltpu.VMEM(groups, F32),
            pltpu.VMEM(groups, F32),
            pltpu.VMEM(groups, F32),
            pltpu.VMEM(groups, F32),
            pltpu.VMEM((28, 8, 128), F32),
            dma((3,)), dma((8,)), dma((2,)), dma((2,)), dma((3,)), dma((3,)),
            dma((n,)), dma((n,)), dma((n,)), dma((n,)), dma((3,)), dma((3,)),
            dma((7,)), dma((7,)), dma((7,)), dma((7,)), dma((7,)), dma((7,)),
        ],
        compiler_params=pltpu.CompilerParams(
            collective_id=0, has_side_effects=True, vmem_limit_bytes=40 << 20
        ),
        name="exchange",
    )(*[pltpu.with_memory_space_constraint(x, pltpu.HBM) for x in (velocity_u, wall_strain, damping, high, low)])
    return pl.pallas_call(
        finish,
        out_shape=[jax.ShapeDtypeStruct(block, F32)] * 3,
        in_specs=[vmem] * 4,
        out_specs=[anywhere] * 3,
        scratch_shapes=[pltpu.VMEM(block, F32), pltpu.VMEM(block, F32), dma((6,))],
        compiler_params=pltpu.CompilerParams(vmem_limit_bytes=16 << 20),
        name="finish",
    )(*between)


def solution(mesh):
    spec = P("gx", None, "gy")
    return jax.shard_map(
        body,
        mesh=mesh,
        in_specs=(spec, spec, P(None, "gy")),
        out_specs=(spec, spec, spec),
        check_vma=False,
    )
```

```python
import functools
import math

import jax
import jax.numpy as jnp
import ml_dtypes
import numpy as np
from jax import lax
from jax.experimental import pallas as pl
from jax.experimental.pallas import tpu as pltpu
from jax.sharding import PartitionSpec as P

MESH = pl.DeviceIdType.MESH
NY = 2048
GY = 4
CELLS = 64
PLANES = 16
COLS = 512
OWN = CELLS // GY
ROUNDS = (1, 2, 0, 3)
STEP = OWN // len(ROUNDS)
PIECE = STEP // 2
F32 = jnp.float32
BF16 = jnp.bfloat16


@functools.cache
def cosine_tables():
    n = np.arange(NY, dtype=np.int64)
    phase = (2 * n[:, None] + 1) * n[None, :] % (4 * NY)
    table = math.sqrt(2.0 / NY) * np.cos(np.pi * phase.astype(np.float64) / (2.0 * NY))
    high = table.astype(ml_dtypes.bfloat16)
    low = (table - high.astype(np.float64)).astype(ml_dtypes.bfloat16)
    return high, low


def split(value):
    high = value.astype(BF16)
    return high, (value - high.astype(F32)).astype(BF16)


def response(damping, doublings):
    power, gain = damping * damping, damping * (1.0 + damping * damping)
    for _ in range(doublings - 1):
        power = power * power
        gain = gain * (1.0 + power)
    scale = damping
    for _ in range(doublings):
        scale = scale * scale
    return scale, gain


def weight_of(damping):
    v = (1.0 - damping) * (1.0 + damping)
    return v * jnp.sqrt(v)


def kernel(
    u_hbm, w_hbm, damping_hbm, high_hbm, low_hbm,
    second, coeffs, factors, carried,
    u, w, damping, source, rows, modes, table_hi, table_lo, lhs,
    halo, damp_tiles, all_damping, all_weight, sub, partial, arrived, lines, gathered, slabs, back, small,
    load_sem, table_sem, halo_send, halo_recv, damp_send, damp_recv, share_send, share_recv, row_send, row_recv, mode_send, mode_recv,
    part_send, part_recv, a_send, a_recv, b_send, b_recv, c_send, c_recv,
):
    gx, gy = lax.axis_index("gx"), lax.axis_index("gy")
    z, member = gx // 8, lax.rem(gx, 8)

    def over_gy(d):
        return {"gy": lax.rem(gy + d, GY)}

    def in_slab(d):
        return {"gx": z * 8 + lax.rem(member + d, 8)}

    def over_z(d):
        return {"gx": lax.rem(z + d, 8) * 8 + member}

    following, previous = {"gx": lax.rem(gx + 1, 64)}, {"gx": lax.rem(gx + 63, 64)}
    out_up, out_down = jnp.logical_and(member == 7, z < 7), jnp.logical_and(member == 0, z > 0)
    barrier = pltpu.get_barrier_semaphore()

    def greet(peer):
        pl.semaphore_signal(barrier, inc=1, device_id=peer, device_id_type=MESH)

    for d in range(1, GY):
        greet(over_gy(d))
    for d in range(1, 8):
        greet(in_slab(d))
    for d in range(1, 8):
        greet(over_z(d))
    for needed, peer in ((out_up, following), (out_down, previous)):

        @pl.when(needed)
        def _(peer=peer):
            greet(peer)

    greeted = 17 + out_up.astype(jnp.int32) + out_down.astype(jnp.int32)

    loads = [
        pltpu.make_async_copy(u_hbm, u, load_sem.at[0]),
        pltpu.make_async_copy(w_hbm, w, load_sem.at[1]),
        pltpu.make_async_copy(damping_hbm, damping, load_sem.at[2]),
    ]
    tables = []
    for d in range(GY):
        block = pl.ds(pl.multiple_of(lax.rem(gy + GY - d, GY) * COLS, COLS), COLS)
        here = pl.ds(d * COLS, COLS)
        tables.append(pltpu.make_async_copy(high_hbm.at[block], table_hi.at[here], table_sem.at[2 * d]))
        tables.append(pltpu.make_async_copy(low_hbm.at[block], table_lo.at[here], table_sem.at[2 * d + 1]))
    for copy in loads:
        copy.start()

    started = []

    def remote(src, dst, send, recv, peer):
        copy = pltpu.make_async_remote_copy(
            src_ref=src, dst_ref=dst, send_sem=send, recv_sem=recv, device_id=peer, device_id_type=MESH
        )
        copy.start()
        started.append(copy)
        return copy

    def stencil(at, i):
        m3, m2, m1, c, p1, p2, p3 = [at(k) for k in range(-3, 4)]
        first = 0.75 * (p1 - m1) - 0.15 * (p2 - m2) + (1.0 / 60.0) * (p3 - m3)
        source[i] = first + w[i]
        second[i] = 1.5 * (p1 + m1) - 0.15 * (p2 + m2) + (1.0 / 90.0) * (p3 + m3) - (49.0 / 18.0) * c

    def inner_chunk(q):
        def step(i, carry):
            stencil(lambda k: u[i + k], i)
            return carry

        for j in range(GY):
            lax.fori_loop(max(j * OWN + q * STEP, 3), min(j * OWN + q * STEP + STEP, CELLS - 3), step, 0)

    row_copies, mode_copies = {}, {}

    def send_rows(q):
        for half in range(2):
            at = q * STEP + half * PIECE
            for d in range(1, GY):
                k = ((d - 1) * len(ROUNDS) + q) * 2 + half
                src = source.at[pl.ds(lax.rem(gy + d, GY) * OWN + at, PIECE)]
                dst = rows.at[d - 1, pl.ds(at, PIECE)]
                row_copies[d, q, half] = remote(src, dst, row_send.at[k], row_recv.at[k], over_gy(d))

    def send_modes(q):
        for half in range(2):
            at = q * STEP + half * PIECE
            for d in range(1, GY):
                k = ((d - 1) * len(ROUNDS) + q) * 2 + half
                src = modes.at[lax.rem(gy + d, GY), pl.ds(at, PIECE)]
                dst = coeffs.at[pl.ds(gy * OWN + at, PIECE)]
                mode_copies[d, q, half] = remote(src, dst, mode_send.at[k], mode_recv.at[k], over_gy(d))

    height = STEP * PLANES

    def transform(q):
        for d in range(GY):
            if d:
                row_copies[d, q, 0].wait_recv()
                row_copies[d, q, 1].wait_recv()
                part = rows[d - 1, q * STEP : (q + 1) * STEP]
            else:
                part = source[pl.ds(gy * OWN + q * STEP, STEP)]
            hi, lo = split(part.reshape(height, COLS))
            lhs[:height, d * COLS : (d + 1) * COLS] = hi
            lhs[height:, d * COLS : (d + 1) * COLS] = lo

        def columns(j, carry):
            at = pl.ds(pl.multiple_of(j * 256, 256), 256)
            both = jnp.dot(lhs[...], table_hi[:, at], preferred_element_type=F32)
            cross = jnp.dot(lhs[:height], table_lo[:, at], preferred_element_type=F32)
            total = both[:height] + both[height:] + cross
            modes[j // 2, q * STEP : (q + 1) * STEP, :, pl.ds(pl.multiple_of(lax.rem(j, 2) * 256, 256), 256)] = (
                total.reshape(STEP, PLANES, 256)
            )
            return carry

        lax.fori_loop(0, NY // 256, columns, 0, unroll=2)
        coeffs[pl.ds(gy * OWN + q * STEP, STEP)] = modes[gy, q * STEP : (q + 1) * STEP]

    r0, r1, r2, r3 = ROUNDS
    loads[0].wait()
    loads[1].wait()
    loads[2].wait()
    for copy in tables:
        copy.start()
    inner_chunk(r0)
    lam = damping[...]
    factors[0] = lam
    factors[1] = weight_of(lam)
    for g in range(8):
        small[g] = lam[8 * (g // 4) : 8 * (g // 4) + 8, 128 * (g % 4) : 128 * (g % 4) + 128]
    damp_tiles[member, gy] = small[member]
    pl.semaphore_wait(barrier, greeted)

    def halo_copy(k):
        src = u.at[pl.ds((CELLS - 3) * (1 - k), 3)]
        peer = (following, previous)[k]
        return pltpu.make_async_remote_copy(
            src_ref=src, dst_ref=halo.at[k], send_sem=halo_send.at[k], recv_sem=halo_recv.at[k],
            device_id=peer, device_id_type=MESH,
        )

    has_next, has_previous = gx < 63, gx > 0

    @pl.when(has_next)
    def _():
        halo_copy(0).start()

    @pl.when(has_previous)
    def _():
        halo_copy(1).start()

    own_tile = damp_tiles.at[member, gy]
    damps = [remote(own_tile, own_tile, damp_send.at[d - 1], damp_recv.at[d - 1], over_gy(d)) for d in range(1, GY)]
    send_rows(r0)
    inner_chunk(r1)
    send_rows(r1)
    inner_chunk(r2)
    inner_chunk(r3)

    @pl.when(has_previous)
    def _():
        halo_copy(0).wait_recv()
        halo_copy(1).wait_send()

    @pl.when(jnp.logical_not(has_previous))
    def _():
        halo[0] = jnp.zeros((3, PLANES, COLS), F32)

    @pl.when(has_next)
    def _():
        halo_copy(1).wait_recv()
        halo_copy(0).wait_send()

    @pl.when(jnp.logical_not(has_next))
    def _():
        halo[1] = jnp.zeros((3, PLANES, COLS), F32)

    def edge(i):
        def at(k):
            j = i + k
            if j < 0:
                return halo[0, j + 3]
            if j >= CELLS:
                return halo[1, j - CELLS]
            return u[j]

        stencil(at, i)

    for i in (0, 1, 2):
        edge(i)
    send_rows(r2)
    for i in (CELLS - 3, CELLS - 2, CELLS - 1):
        edge(i)
    send_rows(r3)
    for copy in damps:
        copy.wait_recv()
    own_group = damp_tiles.at[member]
    shares = [remote(own_group, own_group, share_send.at[d - 1], share_recv.at[d - 1], in_slab(d)) for d in range(1, 8)]

    for k, value in enumerate(response(lam, 4)):
        sub[k] = value
    for k, value in enumerate((*response(small[member], 6), *response(small[member], 9))):
        small[8 + k] = value
    for copy in shares:
        copy.wait_recv()
    for o in range(GY):
        for g in range(8):
            at = slice(8 * (g // 4), 8 * (g // 4) + 8), slice(128 * (g % 4), 128 * (g % 4) + 128)
            all_damping[(o, *at)] = damp_tiles[g, o]
        all_weight[o] = weight_of(all_damping[o])
    for copy in tables:
        copy.wait()

    transform(r0)
    send_modes(r0)
    transform(r1)
    transform(r2)
    transform(r3)

    blank = jnp.zeros((PLANES, COLS), F32)
    for o in range(GY):

        def own_rows(i, carry, o=o):
            s, t, power = carry
            s = all_weight[o] * modes[o, i] + all_damping[o] * s
            return s, t + power * s, power * all_damping[o]

        s, t, _ = lax.fori_loop(0, OWN, own_rows, (blank, blank, blank + 1.0), unroll=2)
        partial[o, 0] = s
        partial[o, 1] = t
    parts = [
        remote(
            partial.at[lax.rem(gy + d, GY)], arrived.at[gy], part_send.at[d - 1], part_recv.at[d - 1],
            over_gy(d),
        )
        for d in range(1, GY)
    ]
    arrived[gy] = partial[gy]
    send_modes(r1)
    send_modes(r2)

    for copy in parts:
        copy.wait_recv()
    s, seen = blank, []
    for j in range(GY):
        seen.append(s)
        s = sub[0] * s + arrived[j, 0]
    t = blank
    for j in reversed(range(GY)):
        t = arrived[j, 1] + sub[1] * seen[j] + sub[0] * t
    for g in range(8):
        at = slice(8 * (g // 4), 8 * (g // 4) + 8), slice(128 * (g % 4), 128 * (g % 4) + 128)
        lines[g, 0] = s[at]
        lines[g, 1] = t[at]

    a_copies = [
        remote(lines.at[lax.rem(member + d, 8)], gathered.at[member], a_send.at[d - 1], a_recv.at[d - 1], in_slab(d))
        for d in range(1, 8)
    ]
    gathered[member] = lines[member]
    send_modes(r3)
    for copy in a_copies:
        copy.wait_recv()
    scale, answer, slab_scale, slab_answer = [small[8 + k] for k in range(4)]
    tile = jnp.zeros((8, 128), F32)
    s_slab, seen = tile, []
    for m in range(8):
        seen.append(s_slab)
        s_slab = scale * s_slab + gathered[m, 0]
    t_slab = tile
    for m in reversed(range(8)):
        t_slab = gathered[m, 1] + answer * seen[m] + scale * t_slab
    slabs[z, 0] = s_slab
    slabs[z, 1] = t_slab
    b_copies = [
        remote(slabs.at[z], slabs.at[z], b_send.at[d - 1], b_recv.at[d - 1], over_z(d)) for d in range(1, 8)
    ]
    for copy in b_copies:
        copy.wait_recv()
    f, seen = tile, []
    for k in range(8):
        seen.append(f)
        small[12 + k] = f
        f = slab_scale * f + slabs[k, 0]
    p = tile
    for k in reversed(range(8)):
        small[20 + k] = p
        p = slabs[k, 1] + slab_answer * seen[k] + slab_scale * p
    f, p = small[12 + z], small[20 + z]
    seen = []
    for m in range(8):
        seen.append(f)
        back[m, 0] = f
        f = scale * f + gathered[m, 0]
    for m in reversed(range(8)):
        back[m, 1] = p
        p = gathered[m, 1] + answer * seen[m] + scale * p
    c_copies = [
        remote(back.at[lax.rem(member + d, 8)], carried.at[member], c_send.at[d - 1], c_recv.at[d - 1], in_slab(d))
        for d in range(1, 8)
    ]
    carried[member] = back[member]
    for copy in c_copies:
        copy.wait_recv()
    for copy in mode_copies.values():
        copy.wait_recv()

    for copy in started:
        copy.wait_send()


def finish(second, coeffs, factors, carried, second_out, coeffs_out, pressure_out, forward, pressure, sem):
    whole = [
        pltpu.make_async_copy(coeffs, coeffs_out, sem.at[0]),
        pltpu.make_async_copy(second, second_out, sem.at[1]),
    ]
    for copy in whole:
        copy.start()
    lam, weight = factors[0], factors[1]

    def joined(which):
        halves = [jnp.concatenate([carried[4 * h + g, which] for g in range(4)], axis=1) for h in range(2)]
        return jnp.concatenate(halves, axis=0)

    def ahead(i, value):
        value = weight * coeffs[i] + lam * value
        forward[i] = value
        return value

    lax.fori_loop(0, CELLS, ahead, joined(0), unroll=4)
    value, quarter = joined(1), CELLS // 4
    for part in reversed(range(4)):

        def behind(i, value):
            k = (part + 1) * quarter - 1 - i
            value = forward[k] + lam * value
            pressure[k] = value
            return value

        value = lax.fori_loop(0, quarter, behind, value, unroll=4)
        here = pl.ds(part * quarter, quarter)
        copy = pltpu.make_async_copy(pressure.at[here], pressure_out.at[here], sem.at[2 + part])
        copy.start()
        whole.append(copy)
    for copy in whole:
        copy.wait()


def body(velocity_u, wall_strain, damping):
    high, low = (jnp.asarray(table) for table in cosine_tables())
    block, plane = (CELLS, PLANES, COLS), (PLANES, COLS)
    vmem = pl.BlockSpec(memory_space=pltpu.VMEM)
    anywhere = pl.BlockSpec(memory_space=pltpu.HBM)
    dma = pltpu.SemaphoreType.DMA
    n, groups = 6 * len(ROUNDS), (8, 2, 8, 128)
    between = pl.pallas_call(
        kernel,
        out_shape=[pltpu.VMEM(shape, F32) for shape in (block, block, (2, *plane), groups)],
        in_specs=[anywhere] * 5,
        out_specs=[vmem] * 4,
        scratch_shapes=[
            pltpu.VMEM(block, F32),
            pltpu.VMEM(block, F32),
            pltpu.VMEM(plane, F32),
            pltpu.VMEM(block, F32),
            pltpu.VMEM((GY - 1, OWN, *plane), F32),
            pltpu.VMEM((GY, OWN, *plane), F32),
            pltpu.VMEM((NY, NY), BF16),
            pltpu.VMEM((NY, NY), BF16),
            pltpu.VMEM((2 * STEP * PLANES, NY), BF16),
            pltpu.VMEM((2, 3, *plane), F32),
            pltpu.VMEM((8, GY, 8, 128), F32),
            pltpu.VMEM((GY, *plane), F32),
            pltpu.VMEM((GY, *plane), F32),
            pltpu.VMEM((2, *plane), F32),
            pltpu.VMEM((GY, 2, *plane), F32),
            pltpu.VMEM((GY, 2, *plane), F32),
            pltpu.VMEM(groups, F32),
            pltpu.VMEM(groups, F32),
            pltpu.VMEM(groups, F32),
            pltpu.VMEM(groups, F32),
            pltpu.VMEM((28, 8, 128), F32),
            dma((3,)), dma((8,)), dma((2,)), dma((2,)), dma((3,)), dma((3,)), dma((7,)), dma((7,)),
            dma((n,)), dma((n,)), dma((n,)), dma((n,)), dma((3,)), dma((3,)),
            dma((7,)), dma((7,)), dma((7,)), dma((7,)), dma((7,)), dma((7,)),
        ],
        compiler_params=pltpu.CompilerParams(
            collective_id=0, has_side_effects=True, vmem_limit_bytes=40 << 20
        ),
        name="exchange",
    )(*[pltpu.with_memory_space_constraint(x, pltpu.HBM) for x in (velocity_u, wall_strain, damping, high, low)])
    return pl.pallas_call(
        finish,
        out_shape=[jax.ShapeDtypeStruct(block, F32)] * 3,
        in_specs=[vmem] * 4,
        out_specs=[anywhere] * 3,
        scratch_shapes=[pltpu.VMEM(block, F32), pltpu.VMEM(block, F32), dma((6,))],
        compiler_params=pltpu.CompilerParams(vmem_limit_bytes=16 << 20),
        name="finish",
    )(*between)


def solution(mesh):
    spec = P("gx", None, "gy")
    return jax.shard_map(
        body,
        mesh=mesh,
        in_specs=(spec, spec, P(None, "gy")),
        out_specs=(spec, spec, spec),
        check_vma=False,
    )
```

```python
import functools
import math

import jax
import jax.numpy as jnp
import ml_dtypes
import numpy as np
from jax import lax
from jax.experimental import pallas as pl
from jax.experimental.pallas import tpu as pltpu
from jax.sharding import PartitionSpec as P

MESH = pl.DeviceIdType.MESH
NY = 2048
GY = 4
CELLS = 64
PLANES = 16
COLS = 512
OWN = CELLS // GY
ROUNDS = (1, 2, 0, 3)
STEP = OWN // len(ROUNDS)
PIECE = STEP // 2
F32 = jnp.float32
BF16 = jnp.bfloat16


@functools.cache
def cosine_tables():
    n = np.arange(NY, dtype=np.int64)
    phase = (2 * n[:, None] + 1) * n[None, :] % (4 * NY)
    table = math.sqrt(2.0 / NY) * np.cos(np.pi * phase.astype(np.float64) / (2.0 * NY))
    high = table.astype(ml_dtypes.bfloat16)
    low = (table - high.astype(np.float64)).astype(ml_dtypes.bfloat16)
    return high, low


def split(value):
    high = value.astype(BF16)
    return high, (value - high.astype(F32)).astype(BF16)


def response(damping, doublings):
    power, gain = damping * damping, damping * (1.0 + damping * damping)
    for _ in range(doublings - 1):
        power = power * power
        gain = gain * (1.0 + power)
    scale = damping
    for _ in range(doublings):
        scale = scale * scale
    return scale, gain


def weight_of(damping):
    v = (1.0 - damping) * (1.0 + damping)
    return v * jnp.sqrt(v)


def kernel(
    u_hbm, w_hbm, damping_hbm, high_hbm, low_hbm,
    second, coeffs, factors, carried,
    u, w, damping, source, rows, modes, table_hi, table_lo, lhs,
    halo, damp_tiles, all_damping, all_weight, sub, partial, arrived, lines, gathered, slabs, back, small,
    load_sem, table_sem, halo_send, halo_recv, damp_send, damp_recv, share_send, share_recv, row_send, row_recv, mode_send, mode_recv,
    part_send, part_recv, a_send, a_recv, b_send, b_recv, c_send, c_recv,
):
    gx, gy = lax.axis_index("gx"), lax.axis_index("gy")
    z, member = gx // 8, lax.rem(gx, 8)

    def over_gy(d):
        return {"gy": lax.rem(gy + d, GY)}

    def in_slab(d):
        return {"gx": z * 8 + lax.rem(member + d, 8)}

    def over_z(d):
        return {"gx": lax.rem(z + d, 8) * 8 + member}

    following, previous = {"gx": lax.rem(gx + 1, 64)}, {"gx": lax.rem(gx + 63, 64)}
    out_up, out_down = jnp.logical_and(member == 7, z < 7), jnp.logical_and(member == 0, z > 0)
    barrier = pltpu.get_barrier_semaphore()

    def greet(peer):
        pl.semaphore_signal(barrier, inc=1, device_id=peer, device_id_type=MESH)

    for d in range(1, GY):
        greet(over_gy(d))
    for d in range(1, 8):
        greet(in_slab(d))
    for d in range(1, 8):
        greet(over_z(d))
    for needed, peer in ((out_up, following), (out_down, previous)):

        @pl.when(needed)
        def _(peer=peer):
            greet(peer)

    greeted = 17 + out_up.astype(jnp.int32) + out_down.astype(jnp.int32)

    loads = [
        pltpu.make_async_copy(u_hbm, u, load_sem.at[0]),
        pltpu.make_async_copy(damping_hbm, damping, load_sem.at[1]),
    ]
    strain = {}
    for q in ROUNDS:
        for j in range(GY):
            here = pl.ds(j * OWN + q * STEP, STEP)
            strain[q, j] = pltpu.make_async_copy(w_hbm.at[here], w.at[here], load_sem.at[2 + q * GY + j])
    loads += [strain[ROUNDS[0], j] for j in range(GY)]
    tables = []
    for d in range(GY):
        block = pl.ds(pl.multiple_of(lax.rem(gy + GY - d, GY) * COLS, COLS), COLS)
        here = pl.ds(d * COLS, COLS)
        tables.append(pltpu.make_async_copy(high_hbm.at[block], table_hi.at[here], table_sem.at[2 * d]))
        tables.append(pltpu.make_async_copy(low_hbm.at[block], table_lo.at[here], table_sem.at[2 * d + 1]))
    for copy in loads:
        copy.start()

    started = []

    def remote(src, dst, send, recv, peer):
        copy = pltpu.make_async_remote_copy(
            src_ref=src, dst_ref=dst, send_sem=send, recv_sem=recv, device_id=peer, device_id_type=MESH
        )
        copy.start()
        started.append(copy)
        return copy

    def stencil(at, i):
        m3, m2, m1, c, p1, p2, p3 = [at(k) for k in range(-3, 4)]
        first = 0.75 * (p1 - m1) - 0.15 * (p2 - m2) + (1.0 / 60.0) * (p3 - m3)
        source[i] = first + w[i]
        second[i] = 1.5 * (p1 + m1) - 0.15 * (p2 + m2) + (1.0 / 90.0) * (p3 + m3) - (49.0 / 18.0) * c

    def inner_chunk(q):
        def step(i, carry):
            stencil(lambda k: u[i + k], i)
            return carry

        for j in range(GY):
            lax.fori_loop(max(j * OWN + q * STEP, 3), min(j * OWN + q * STEP + STEP, CELLS - 3), step, 0)

    row_copies, mode_copies = {}, {}

    def send_rows(q):
        for half in range(2):
            at = q * STEP + half * PIECE
            for d in range(1, GY):
                k = ((d - 1) * len(ROUNDS) + q) * 2 + half
                src = source.at[pl.ds(lax.rem(gy + d, GY) * OWN + at, PIECE)]
                dst = rows.at[d - 1, pl.ds(at, PIECE)]
                row_copies[d, q, half] = remote(src, dst, row_send.at[k], row_recv.at[k], over_gy(d))

    def send_modes(q):
        for half in range(2):
            at = q * STEP + half * PIECE
            for d in range(1, GY):
                k = ((d - 1) * len(ROUNDS) + q) * 2 + half
                src = modes.at[lax.rem(gy + d, GY), pl.ds(at, PIECE)]
                dst = coeffs.at[pl.ds(gy * OWN + at, PIECE)]
                mode_copies[d, q, half] = remote(src, dst, mode_send.at[k], mode_recv.at[k], over_gy(d))

    height = STEP * PLANES

    def transform(q):
        for d in range(GY):
            if d:
                row_copies[d, q, 0].wait_recv()
                row_copies[d, q, 1].wait_recv()
                part = rows[d - 1, q * STEP : (q + 1) * STEP]
            else:
                part = source[pl.ds(gy * OWN + q * STEP, STEP)]
            hi, lo = split(part.reshape(height, COLS))
            lhs[:height, d * COLS : (d + 1) * COLS] = hi
            lhs[height:, d * COLS : (d + 1) * COLS] = lo

        def columns(j, carry):
            at = pl.ds(pl.multiple_of(j * 256, 256), 256)
            both = jnp.dot(lhs[...], table_hi[:, at], preferred_element_type=F32)
            cross = jnp.dot(lhs[:height], table_lo[:, at], preferred_element_type=F32)
            total = both[:height] + both[height:] + cross
            modes[j // 2, q * STEP : (q + 1) * STEP, :, pl.ds(pl.multiple_of(lax.rem(j, 2) * 256, 256), 256)] = (
                total.reshape(STEP, PLANES, 256)
            )
            return carry

        lax.fori_loop(0, NY // 256, columns, 0, unroll=2)
        coeffs[pl.ds(gy * OWN + q * STEP, STEP)] = modes[gy, q * STEP : (q + 1) * STEP]

    r0, r1, r2, r3 = ROUNDS
    for copy in loads:
        copy.wait()
    others = [strain[q, j] for q in ROUNDS[1:] for j in range(GY)]
    for copy in others + tables:
        copy.start()
    inner_chunk(r0)
    lam = damping[...]
    factors[0] = lam
    factors[1] = weight_of(lam)
    for g in range(8):
        small[g] = lam[8 * (g // 4) : 8 * (g // 4) + 8, 128 * (g % 4) : 128 * (g % 4) + 128]
    damp_tiles[member, gy] = small[member]
    pl.semaphore_wait(barrier, greeted)

    def halo_copy(k):
        src = u.at[pl.ds((CELLS - 3) * (1 - k), 3)]
        peer = (following, previous)[k]
        return pltpu.make_async_remote_copy(
            src_ref=src, dst_ref=halo.at[k], send_sem=halo_send.at[k], recv_sem=halo_recv.at[k],
            device_id=peer, device_id_type=MESH,
        )

    has_next, has_previous = gx < 63, gx > 0

    @pl.when(has_next)
    def _():
        halo_copy(0).start()

    @pl.when(has_previous)
    def _():
        halo_copy(1).start()

    own_tile = damp_tiles.at[member, gy]
    damps = [remote(own_tile, own_tile, damp_send.at[d - 1], damp_recv.at[d - 1], over_gy(d)) for d in range(1, GY)]
    send_rows(r0)
    for copy in others:
        copy.wait()
    inner_chunk(r1)
    send_rows(r1)
    inner_chunk(r2)
    inner_chunk(r3)

    @pl.when(has_previous)
    def _():
        halo_copy(0).wait_recv()
        halo_copy(1).wait_send()

    @pl.when(jnp.logical_not(has_previous))
    def _():
        halo[0] = jnp.zeros((3, PLANES, COLS), F32)

    @pl.when(has_next)
    def _():
        halo_copy(1).wait_recv()
        halo_copy(0).wait_send()

    @pl.when(jnp.logical_not(has_next))
    def _():
        halo[1] = jnp.zeros((3, PLANES, COLS), F32)

    def edge(i):
        def at(k):
            j = i + k
            if j < 0:
                return halo[0, j + 3]
            if j >= CELLS:
                return halo[1, j - CELLS]
            return u[j]

        stencil(at, i)

    for i in (0, 1, 2):
        edge(i)
    send_rows(r2)
    for i in (CELLS - 3, CELLS - 2, CELLS - 1):
        edge(i)
    send_rows(r3)
    for copy in damps:
        copy.wait_recv()
    own_group = damp_tiles.at[member]
    shares = [remote(own_group, own_group, share_send.at[d - 1], share_recv.at[d - 1], in_slab(d)) for d in range(1, 8)]

    for k, value in enumerate(response(lam, 4)):
        sub[k] = value
    for k, value in enumerate((*response(small[member], 6), *response(small[member], 9))):
        small[8 + k] = value
    for copy in shares:
        copy.wait_recv()
    for o in range(GY):
        for g in range(8):
            at = slice(8 * (g // 4), 8 * (g // 4) + 8), slice(128 * (g % 4), 128 * (g % 4) + 128)
            all_damping[(o, *at)] = damp_tiles[g, o]
        all_weight[o] = weight_of(all_damping[o])
    for copy in tables:
        copy.wait()

    transform(r0)
    send_modes(r0)
    transform(r1)
    transform(r2)
    transform(r3)

    blank = jnp.zeros((PLANES, COLS), F32)
    parts = []
    for d in (1, 2, 3, 0):
        o = lax.rem(gy + d, GY)

        def own_rows(i, carry, o=o):
            s, t, power = carry
            s = all_weight[o] * modes[o, i] + all_damping[o] * s
            return s, t + power * s, power * all_damping[o]

        s, t, _ = lax.fori_loop(0, OWN, own_rows, (blank, blank, blank + 1.0), unroll=2)
        if d:
            partial[o, 0] = s
            partial[o, 1] = t
            parts.append(remote(partial.at[o], arrived.at[gy], part_send.at[d - 1], part_recv.at[d - 1], over_gy(d)))
        else:
            arrived[gy, 0] = s
            arrived[gy, 1] = t
    send_modes(r1)
    send_modes(r2)

    for copy in parts:
        copy.wait_recv()
    s, seen = blank, []
    for j in range(GY):
        seen.append(s)
        s = sub[0] * s + arrived[j, 0]
    t = blank
    for j in reversed(range(GY)):
        t = arrived[j, 1] + sub[1] * seen[j] + sub[0] * t
    for g in range(8):
        at = slice(8 * (g // 4), 8 * (g // 4) + 8), slice(128 * (g % 4), 128 * (g % 4) + 128)
        lines[g, 0] = s[at]
        lines[g, 1] = t[at]

    a_copies = [
        remote(lines.at[lax.rem(member + d, 8)], gathered.at[member], a_send.at[d - 1], a_recv.at[d - 1], in_slab(d))
        for d in range(1, 8)
    ]
    gathered[member] = lines[member]
    send_modes(r3)
    for copy in a_copies:
        copy.wait_recv()
    scale, answer, slab_scale, slab_answer = [small[8 + k] for k in range(4)]
    tile = jnp.zeros((8, 128), F32)
    s_slab, seen = tile, []
    for m in range(8):
        seen.append(s_slab)
        s_slab = scale * s_slab + gathered[m, 0]
    t_slab = tile
    for m in reversed(range(8)):
        t_slab = gathered[m, 1] + answer * seen[m] + scale * t_slab
    slabs[z, 0] = s_slab
    slabs[z, 1] = t_slab
    b_copies = [
        remote(slabs.at[z], slabs.at[z], b_send.at[d - 1], b_recv.at[d - 1], over_z(d)) for d in range(1, 8)
    ]
    for copy in b_copies:
        copy.wait_recv()
    f, seen = tile, []
    for k in range(8):
        seen.append(f)
        small[12 + k] = f
        f = slab_scale * f + slabs[k, 0]
    p = tile
    for k in reversed(range(8)):
        small[20 + k] = p
        p = slabs[k, 1] + slab_answer * seen[k] + slab_scale * p
    f, p = small[12 + z], small[20 + z]
    seen = []
    for m in range(8):
        seen.append(f)
        back[m, 0] = f
        f = scale * f + gathered[m, 0]
    for m in reversed(range(8)):
        back[m, 1] = p
        p = gathered[m, 1] + answer * seen[m] + scale * p
    c_copies = [
        remote(back.at[lax.rem(member + d, 8)], carried.at[member], c_send.at[d - 1], c_recv.at[d - 1], in_slab(d))
        for d in range(1, 8)
    ]
    carried[member] = back[member]
    for copy in c_copies:
        copy.wait_recv()
    for copy in mode_copies.values():
        copy.wait_recv()

    for copy in started:
        copy.wait_send()


def finish(second, coeffs, factors, carried, second_out, coeffs_out, pressure_out, forward, pressure, sem):
    whole = [
        pltpu.make_async_copy(coeffs, coeffs_out, sem.at[0]),
        pltpu.make_async_copy(second, second_out, sem.at[1]),
    ]
    for copy in whole:
        copy.start()
    lam, weight = factors[0], factors[1]

    def joined(which):
        halves = [jnp.concatenate([carried[4 * h + g, which] for g in range(4)], axis=1) for h in range(2)]
        return jnp.concatenate(halves, axis=0)

    def ahead(i, value):
        value = weight * coeffs[i] + lam * value
        forward[i] = value
        return value

    lax.fori_loop(0, CELLS, ahead, joined(0), unroll=4)
    value, quarter = joined(1), CELLS // 4
    for part in reversed(range(4)):

        def behind(i, value):
            k = (part + 1) * quarter - 1 - i
            value = forward[k] + lam * value
            pressure[k] = value
            return value

        value = lax.fori_loop(0, quarter, behind, value, unroll=4)
        here = pl.ds(part * quarter, quarter)
        copy = pltpu.make_async_copy(pressure.at[here], pressure_out.at[here], sem.at[2 + part])
        copy.start()
        whole.append(copy)
    for copy in whole:
        copy.wait()


def body(velocity_u, wall_strain, damping):
    high, low = (jnp.asarray(table) for table in cosine_tables())
    block, plane = (CELLS, PLANES, COLS), (PLANES, COLS)
    vmem = pl.BlockSpec(memory_space=pltpu.VMEM)
    anywhere = pl.BlockSpec(memory_space=pltpu.HBM)
    dma = pltpu.SemaphoreType.DMA
    n, groups = 6 * len(ROUNDS), (8, 2, 8, 128)
    between = pl.pallas_call(
        kernel,
        out_shape=[pltpu.VMEM(shape, F32) for shape in (block, block, (2, *plane), groups)],
        in_specs=[anywhere] * 5,
        out_specs=[vmem] * 4,
        scratch_shapes=[
            pltpu.VMEM(block, F32),
            pltpu.VMEM(block, F32),
            pltpu.VMEM(plane, F32),
            pltpu.VMEM(block, F32),
            pltpu.VMEM((GY - 1, OWN, *plane), F32),
            pltpu.VMEM((GY, OWN, *plane), F32),
            pltpu.VMEM((NY, NY), BF16),
            pltpu.VMEM((NY, NY), BF16),
            pltpu.VMEM((2 * STEP * PLANES, NY), BF16),
            pltpu.VMEM((2, 3, *plane), F32),
            pltpu.VMEM((8, GY, 8, 128), F32),
            pltpu.VMEM((GY, *plane), F32),
            pltpu.VMEM((GY, *plane), F32),
            pltpu.VMEM((2, *plane), F32),
            pltpu.VMEM((GY, 2, *plane), F32),
            pltpu.VMEM((GY, 2, *plane), F32),
            pltpu.VMEM(groups, F32),
            pltpu.VMEM(groups, F32),
            pltpu.VMEM(groups, F32),
            pltpu.VMEM(groups, F32),
            pltpu.VMEM((28, 8, 128), F32),
            dma((18,)), dma((8,)), dma((2,)), dma((2,)), dma((3,)), dma((3,)), dma((7,)), dma((7,)),
            dma((n,)), dma((n,)), dma((n,)), dma((n,)), dma((3,)), dma((3,)),
            dma((7,)), dma((7,)), dma((7,)), dma((7,)), dma((7,)), dma((7,)),
        ],
        compiler_params=pltpu.CompilerParams(
            collective_id=0, has_side_effects=True, vmem_limit_bytes=40 << 20
        ),
        name="exchange",
    )(*[pltpu.with_memory_space_constraint(x, pltpu.HBM) for x in (velocity_u, wall_strain, damping, high, low)])
    return pl.pallas_call(
        finish,
        out_shape=[jax.ShapeDtypeStruct(block, F32)] * 3,
        in_specs=[vmem] * 4,
        out_specs=[anywhere] * 3,
        scratch_shapes=[pltpu.VMEM(block, F32), pltpu.VMEM(block, F32), dma((6,))],
        compiler_params=pltpu.CompilerParams(vmem_limit_bytes=16 << 20),
        name="finish",
    )(*between)


def solution(mesh):
    spec = P("gx", None, "gy")
    return jax.shard_map(
        body,
        mesh=mesh,
        in_specs=(spec, spec, P(None, "gy")),
        out_specs=(spec, spec, spec),
        check_vma=False,
    )
```
